512 devices in a mesh: dp: 32 (over z, x_hi), lon: 16 (over y, x_lo, core).
Axes of the slice: x: 4 (x_hi: 2, x_lo: 2; x = x_hi * 2 + x_lo), y: 4, z: 16, core: 2. Of those that a mesh axis runs over, the one named last changes fastest.
Arguments:
- fields: bfloat16 [32, 128, 48, 768], P('dp', 'lon'), may hold values from -6 to 6
- cotangent: bfloat16 [32, 128, 48, 768], P('dp', 'lon'), may hold values from -6 to 6
- first_weight: bfloat16 [2, 8, 96, 96], replicated, may hold values from -0.4375 to 0.4375
- second_weight: bfloat16 [2, 8, 96, 96], replicated, may hold values from -0.4375 to 0.4375
Outputs:
- layer_out: bfloat16 [32, 128, 48, 768], P('dp', 'lon')
- field_grad: bfloat16 [32, 128, 48, 768], P('dp', 'lon')
- first_grad: float32 [2, 8, 96, 96], replicated
- second_grad: float32 [2, 8, 96, 96], replicated
The draws below stay inside these ranges and needn't reach their ends.
All inputs are finite; a program needn't handle non-finite values.
Results may differ from the reference program's by a relative error of at most 0.015.
Values may be sent and summed in bfloat16 or wider, within the bound.
A program may use at most 64 MiB of HBM per device.

```python
import math
import jax
import jax.numpy as jnp
from jax import lax

C = 768
NB = 8
CB = 96
W = 128
KM = 64
LAT = 48
SAMPLES = 32


def block_scale(key, shape, pieces, low, top_value):
    loudness, own = 1.0, jax.random.fold_in(key, 6)
    for position, parts in pieces:
        draws = jnp.exp(jax.random.uniform(jax.random.fold_in(own, position), (parts,), jnp.float32, low / len(pieces), top_value / len(pieces)))
        loudness = loudness * jnp.repeat(draws, shape[position] // parts).reshape([-1 if axis == position else 1 for axis in range(len(shape))])
    return loudness


def normal_values(stream_key, extent, scale, reach, split=(), held_as=jnp.bfloat16):
    entries = jax.random.normal(stream_key, extent, jnp.float32) * scale
    if len(split) > 0:
        entries = block_scale(stream_key, extent, split, -0.22, 0.18) * entries
    return jnp.clip(entries, min=-reach, max=reach).astype(held_as)


def setup_inputs(seed: int = 0) -> dict:
    key_list = jax.random.split(jax.random.key(seed), 5)
    fields = normal_values(key_list[0], (SAMPLES, W, LAT, C), 1.0, 6.0, ((0, 32), (1, 16)))
    cotangent = normal_values(key_list[1], (SAMPLES, W, LAT, C), 1.0, 6.0, ((0, 32), (1, 16)))
    first_weight = normal_values(key_list[2], (2, NB, CB, CB), (2 * CB) ** -0.5, 0.4375)
    second_weight = normal_values(key_list[3], (2, NB, CB, CB), (2 * CB) ** -0.5, 0.4375)
    return {"fields": fields, "cotangent": cotangent, "first_weight": first_weight, "second_weight": second_weight}


COEF = 0.7978845608028654
CUBIC = 0.044715

def gelu_value(inner):
    hyper = jnp.tanh(COEF * (inner + CUBIC * inner * inner * inner))
    return 0.5 * inner * (1.0 + hyper)

def gelu_slope(inner):
    hyper = jnp.tanh(COEF * (inner + CUBIC * inner * inner * inner))
    return 0.5 * (1.0 + hyper) + 0.5 * inner * (1.0 - hyper * hyper) * COEF * (1.0 + 3.0 * CUBIC * inner * inner)

def make_basis(length, count):
    cell_idx = jnp.arange(length, dtype=jnp.int32)
    mode_idx = jnp.arange(count, dtype=jnp.int32)
    product = cell_idx[:, None] * mode_idx[None, :] % length
    angle = product.astype(jnp.float32) * jnp.float32(2.0 * math.pi / length)
    return jnp.stack([jnp.cos(angle), -jnp.sin(angle)], axis=-1).astype(jnp.bfloat16)

def lat_mix(part, table):
    return jnp.einsum('khc,hj->kjc', part.astype(jnp.float32), table.astype(jnp.float32))

def lat_forward(spec, lat_basis, lat_scale):
    real_in = spec[:, 0]
    imag_in = spec[:, 1]
    cos_tab = lat_basis[:, :, 0]
    sin_tab = lat_basis[:, :, 1]
    out_r = lat_mix(real_in, cos_tab) - lat_mix(imag_in, sin_tab)
    out_i = lat_mix(imag_in, cos_tab) + lat_mix(real_in, sin_tab)
    return (jnp.stack([out_r, out_i], axis=1) * lat_scale).astype(jnp.bfloat16)

def lat_inverse(spec, lat_basis, lat_scale):
    real_in = spec[:, 0]
    imag_in = spec[:, 1]
    cos_tab = lat_basis[:, :, 0]
    sin_tab = lat_basis[:, :, 1]
    out_r = lat_mix(real_in, cos_tab) + lat_mix(imag_in, sin_tab)
    out_i = lat_mix(imag_in, cos_tab) - lat_mix(real_in, sin_tab)
    return (jnp.stack([out_r, out_i], axis=1) * lat_scale).astype(jnp.bfloat16)

def mat_mul(left, right):
    return jnp.einsum('mhbi,bij->mhbj', left.astype(jnp.float32), right.astype(jnp.float32))

def mat_adj(left, right):
    return jnp.einsum('mhbj,bij->mhbi', left.astype(jnp.float32), right.astype(jnp.float32))

def mat_outer(left, right):
    return jnp.einsum('mhbi,mhbj->bij', left.astype(jnp.float32), right.astype(jnp.float32))

def block_product(real_in, imag_in, weight):
    return (mat_mul(real_in, weight[0]) - mat_mul(imag_in, weight[1]), mat_mul(real_in, weight[1]) + mat_mul(imag_in, weight[0]))

def block_adjoint(real_in, imag_in, weight):
    return (mat_adj(real_in, weight[0]) + mat_adj(imag_in, weight[1]), mat_adj(imag_in, weight[0]) - mat_adj(real_in, weight[1]))

def block_outer(left_r, left_i, right_r, right_i):
    return jnp.stack([mat_outer(left_r, right_r) + mat_outer(left_i, right_i), mat_outer(left_r, right_i) - mat_outer(left_i, right_r)])

def one_sample(pair, first_weight, second_weight):
    field_rows, cot_rows = pair
    dft_basis = make_basis(W, KM).astype(jnp.float32)
    lat_basis = make_basis(LAT, LAT)
    norm_scale = 1.0 / math.sqrt(W)
    lat_scale = 1.0 / math.sqrt(LAT)
    mode_idx = jnp.arange(KM, dtype=jnp.int32)
    mode_weight = jnp.where(mode_idx == 0, 1.0, 2.0).astype(jnp.bfloat16)[:, None, None, None]
    lon_spec = (jnp.einsum('whc,wkp->kphc', field_rows.astype(jnp.float32), dft_basis) * norm_scale).astype(jnp.bfloat16)
    spectrum = lat_forward(lon_spec, lat_basis, lat_scale)
    spec_r = spectrum[:, 0].reshape(KM, LAT, NB, CB)
    spec_i = spectrum[:, 1].reshape(KM, LAT, NB, CB)
    inner_r, inner_i = block_product(spec_r, spec_i, first_weight)
    act_real = gelu_value(inner_r).astype(jnp.bfloat16)
    act_imag = gelu_value(inner_i).astype(jnp.bfloat16)
    out_r, out_i = block_product(act_real, act_imag, second_weight)
    mixed = jnp.stack([out_r.astype(jnp.bfloat16), out_i.astype(jnp.bfloat16)], axis=1).reshape(KM, 2, LAT, C) * mode_weight
    mixed_lon = lat_inverse(mixed, lat_basis, lat_scale)
    wave = (jnp.einsum('kphc,wkp->whc', mixed_lon.astype(jnp.float32), dft_basis) * norm_scale).astype(jnp.bfloat16)
    layer_out = (field_rows.astype(jnp.float32) + wave.astype(jnp.float32)).astype(jnp.bfloat16)
    dual_lon = (jnp.einsum('whc,wkp->kphc', cot_rows.astype(jnp.float32), dft_basis) * norm_scale).astype(jnp.bfloat16)
    dual = lat_forward(dual_lon, lat_basis, lat_scale) * mode_weight
    dual_r = dual[:, 0].reshape(KM, LAT, NB, CB)
    dual_i = dual[:, 1].reshape(KM, LAT, NB, CB)
    back_r, back_i = block_adjoint(dual_r, dual_i, second_weight)
    pre_r = (back_r * gelu_slope(inner_r)).astype(jnp.bfloat16)
    pre_i = (back_i * gelu_slope(inner_i)).astype(jnp.bfloat16)
    bspec_r, bspec_i = block_adjoint(pre_r, pre_i, first_weight)
    back_spec = jnp.stack([bspec_r.astype(jnp.bfloat16), bspec_i.astype(jnp.bfloat16)], axis=1).reshape(KM, 2, LAT, C)
    back_lon = lat_inverse(back_spec, lat_basis, lat_scale)
    pull = (jnp.einsum('kphc,wkp->whc', back_lon.astype(jnp.float32), dft_basis) * norm_scale).astype(jnp.bfloat16)
    field_grad = (cot_rows.astype(jnp.float32) + pull.astype(jnp.float32)).astype(jnp.bfloat16)
    second_term = block_outer(act_real, act_imag, dual_r, dual_i)
    first_term = block_outer(spec_r, spec_i, pre_r, pre_i)
    return (layer_out, field_grad, first_term, second_term)

def reference(fields, cotangent, first_weight, second_weight):

    def run_one(pair):
        return one_sample(pair, first_weight, second_weight)
    layer_out, field_grad, first_terms, second_terms = lax.map(run_one, (fields, cotangent))
    first_grad = lax.optimization_barrier(jnp.sum(first_terms, axis=0)) / SAMPLES
    second_grad = lax.optimization_barrier(jnp.sum(second_terms, axis=0)) / SAMPLES
    return (layer_out, field_grad, first_grad, second_grad)
```

```python
import math

import jax
import jax.numpy as jnp
import ml_dtypes
import numpy as np
from jax import lax
from jax.experimental import pallas as pl
from jax.experimental.pallas import tpu as pltpu
from jax.sharding import PartitionSpec as P

COEF = 0.7978845608028654
CUBIC = 0.044715

SAMPLES = 32
CELLS = 128
LAT = 48
MODES = 64
CHANNELS = 768
GROUPS = 8
WIDTH = 96

LON = 16
ROWS = CELLS // LON
HALF = CHANNELS // 2
PAIRS = LAT // 2
OWN = PAIRS // (LON // 2)
TILE = 2 * ROWS
LINES = OWN * 2 * MODES
TILES = 9
SCALE = 1.0 / math.sqrt(CELLS * LAT)
MESH = pl.DeviceIdType.MESH
BF16 = jnp.bfloat16
F32 = jnp.float32


def make_basis(length, count):
    product = np.arange(length)[:, None] * np.arange(count)[None, :] % length
    angle = product.astype(np.float32) * np.float32(2.0 * math.pi / length)
    table = np.stack([np.cos(angle), -np.sin(angle)], axis=-1)
    return table.astype(ml_dtypes.bfloat16).astype(np.float32)


def lat_matrix():
    table = make_basis(LAT, LAT)
    half = np.zeros((PAIRS, 2, LAT), np.float32)
    half[0, 0] = table[:, 0, 0]
    half[0, 1] = table[:, PAIRS, 0]
    for j in range(1, PAIRS):
        half[j, 0] = table[:, j, 0]
        half[j, 1] = table[:, j, 1]
    full = np.einsum("pah,wv->pawvh", half, np.eye(ROWS, dtype=np.float32))
    return full.reshape(PAIRS * 2 * ROWS, ROWS * LAT)


def lon_matrix(special, weighted):
    table = make_basis(CELLS, MODES)
    cos, sin = table[:, :, 0].T, table[:, :, 1].T
    if weighted:
        factor = np.where(np.arange(MODES) == 0, 1.0, 2.0).astype(np.float32)[:, None]
        cos, sin = cos * factor, sin * factor
    zero = np.zeros_like(cos)
    if special:
        from_real = [cos, sin, zero, zero]
        from_imag = [zero, zero, cos, sin]
    else:
        from_real = [cos, sin, cos, sin]
        from_imag = [-sin, cos, sin, -cos]
    both = np.stack([np.concatenate(from_real), np.concatenate(from_imag)], axis=1)
    both = both.reshape(4 * MODES, 2, LON, ROWS).transpose(0, 2, 1, 3)
    return both.reshape(4 * MODES, 2 * CELLS)


def lon_matrices():
    found = []
    for special in (False, True):
        plain, weighted = lon_matrix(special, False), lon_matrix(special, True)
        found += [plain, weighted, plain.T, weighted.T]
    return np.stack(found)


def matmul(left, right):
    return jnp.dot(left, right, preferred_element_type=F32)


def contract(left, right, axis):
    return lax.dot_general(
        left, right, (((axis,), (axis,)), ((), ())), preferred_element_type=F32
    )


def kernel(
    x_hbm, y_hbm, w1_hbm, w2_hbm, lon_hbm, latf_hbm, lati_hbm,
    outx_hbm, outy_hbm, grad1_hbm, grad2_hbm,
    xv, yv, w1v, w2v, lonv, latf, lati,
    send_x, send_y, recv_x, recv_y, back_x, back_y, home_x, home_y,
    wide1, wide2, place, spec, dual, act, pre, slope, mixed,
    square, grads, part1, own1, part2, own3, final, strip, grad1, grad2,
    load_sem, store_sem, self_sem, out_sem, in_sem,
    sum_out, sum_in, dp_out, dp_in, cast_out, cast_in, gather_out, gather_in,
):
    dp_count = lax.axis_size("dp")
    me, dp = lax.axis_index("lon"), lax.axis_index("dp")

    def half_of(s):
        return lax.rem(s // 2, 2)

    def slot_of(s):
        return (s // 4) * 2 + lax.rem(s, 2)

    def device_of(e, u):
        return (e // 2) * 4 + u * 2 + lax.rem(e, 2)

    u, e = half_of(me), slot_of(me)
    first = jnp.where(e == 0, 4, 0)

    loads = [
        pltpu.make_async_copy(x_hbm, xv, load_sem.at[0]),
        pltpu.make_async_copy(latf_hbm, latf, load_sem.at[1]),
        pltpu.make_async_copy(y_hbm, yv, load_sem.at[2]),
        pltpu.make_async_copy(w1_hbm, w1v, load_sem.at[3]),
        pltpu.make_async_copy(w2_hbm, w2v, load_sem.at[4]),
        pltpu.make_async_copy(lon_hbm.at[pl.ds(0, 4)], lonv.at[pl.ds(0, 4)], load_sem.at[5]),
        pltpu.make_async_copy(lon_hbm.at[pl.ds(first, 4)], lonv.at[pl.ds(4, 4)], load_sem.at[6]),
        pltpu.make_async_copy(lati_hbm, lati, load_sem.at[7]),
    ]
    for load in loads:
        load.start()

    barrier = pltpu.get_barrier_semaphore()

    @pl.loop(1, LON)
    def _(i):
        pl.semaphore_signal(
            barrier, inc=1, device_id=(dp, lax.rem(me + i, LON)), device_id_type=MESH
        )

    @pl.loop(1, dp_count)
    def _(i):
        pl.semaphore_signal(
            barrier, inc=1, device_id=(lax.rem(dp + i, dp_count), me), device_id_type=MESH
        )

    def lat_forward(rows, out):
        for n in range(3):
            lanes = slice(256 * n, 256 * n + 256)
            got = matmul(latf[...], rows[:, lanes]).astype(BF16)
            out[:, :, lanes] = got.reshape(PAIRS, TILE, 256)

    def block_of(buf, s):
        lanes = pl.ds(pl.multiple_of(half_of(s) * HALF, 128), HALF)
        return buf.at[pl.ds(slot_of(s) * OWN, OWN), :, lanes]

    def to_mixer(stage, src, dst, i):
        s = lax.rem(me + i, LON)
        return pltpu.make_async_remote_copy(
            src_ref=block_of(src, s),
            dst_ref=dst.at[:, me],
            send_sem=out_sem.at[stage, i],
            recv_sem=in_sem.at[stage, me],
            device_id=(dp, s),
            device_id_type=MESH,
        )

    def to_cells(stage, src, dst, i):
        s = lax.rem(me + i, LON)
        return pltpu.make_async_remote_copy(
            src_ref=src.at[:, s],
            dst_ref=block_of(dst, me),
            send_sem=out_sem.at[stage, i],
            recv_sem=in_sem.at[stage, me],
            device_id=(dp, s),
            device_id_type=MESH,
        )

    def start_all(make, stage, src, dst):
        @pl.loop(1, LON)
        def _(i):
            make(stage, src, dst, i).start()

    def arrived(stage, buf):
        @pl.loop(1, LON)
        def _(i):
            s = lax.rem(me + i, LON)
            if stage < 2:
                spot = buf.at[:, s]
            else:
                spot = block_of(buf, s)
            pltpu.make_async_remote_copy(
                src_ref=spot,
                dst_ref=spot,
                send_sem=out_sem.at[stage, i],
                recv_sem=in_sem.at[stage, s],
                device_id=(dp, s),
                device_id_type=MESH,
            ).wait_recv()

    def keep_forward(src, dst, n):
        return pltpu.make_async_copy(block_of(src, me), dst.at[:, me], self_sem.at[n])

    def keep_back(src, dst, n):
        return pltpu.make_async_copy(src.at[:, me], block_of(dst, me), self_sem.at[n])

    loads[0].wait()
    loads[1].wait()
    lat_forward(xv, send_x)
    pl.semaphore_wait(barrier, LON - 1 + dp_count - 1)
    start_all(to_mixer, 0, send_x, recv_x)
    keep_x = keep_forward(send_x, recv_x, 0)
    keep_x.start()
    loads[2].wait()
    lat_forward(yv, send_y)
    start_all(to_mixer, 1, send_y, recv_y)
    keep_y = keep_forward(send_y, recv_y, 1)
    keep_y.start()

    def widen(weight, wide):
        for p in range(2):
            for g in range(4):
                own = slice(WIDTH * g, WIDTH * g + WIDTH)
                place[p, own, own] = weight[p, 4 * u + g].astype(F32)
        real, imag = place[0].astype(BF16), place[1].astype(BF16)
        wide[:HALF, :HALF] = real
        wide[HALF:, HALF:] = real
        wide[:HALF, HALF:] = imag
        wide[HALF:, :HALF] = -imag

    place[...] = jnp.zeros_like(place)
    for load in loads[3:]:
        load.wait()
    widen(w1v, wide1)
    widen(w2v, wide2)

    def lon_forward(buf, kind, out):
        for p in range(OWN):
            table = lonv[kind + (4 if p == 0 else 0)]
            got = matmul(table, buf[p].reshape(2 * CELLS, HALF))
            got = (got * SCALE).astype(BF16)
            for x in range(2):
                rows = slice((2 * p + x) * MODES, (2 * p + x + 1) * MODES)
                out[rows, :HALF] = got[2 * x * MODES : (2 * x + 1) * MODES]
                out[rows, HALF:] = got[(2 * x + 1) * MODES : (2 * x + 2) * MODES]

    def store_mixed(got, part):
        for p in range(OWN):
            for x in range(2):
                rows = slice((2 * p + x) * MODES, (2 * p + x + 1) * MODES)
                to = slice((2 * x + part) * MODES, (2 * x + part + 1) * MODES)
                mixed[p, to, :] = got[rows]

    def lon_inverse(kind, out):
        for p in range(OWN):
            table = lonv[kind + (4 if p == 0 else 0)]
            got = matmul(table, mixed[p]).astype(BF16)
            out[p] = got.reshape(LON, TILE, HALF)

    keep_x.wait()
    arrived(0, recv_x)
    lon_forward(recv_x, 0, spec)
    for part in range(2):
        lanes = slice(HALF * part, HALF * part + HALF)
        inner = matmul(spec[...], wide1[:, lanes])
        hyper = jnp.tanh(COEF * (inner + CUBIC * inner * inner * inner))
        act[:, lanes] = (0.5 * inner * (1.0 + hyper)).astype(BF16)
        slope[:, lanes] = 0.5 * (1.0 + hyper) + 0.5 * inner * (1.0 - hyper * hyper) * COEF * (
            1.0 + 3.0 * CUBIC * inner * inner
        )
    for part in range(2):
        lanes = slice(HALF * part, HALF * part + HALF)
        store_mixed(matmul(act[...], wide2[:, lanes]).astype(BF16), part)
    lon_inverse(3, back_x)
    start_all(to_cells, 2, back_x, home_x)
    keep_x = keep_back(back_x, home_x, 2)
    keep_x.start()

    def outer(left, right, n):
        for m in range(6):
            lanes = slice(128 * m, 128 * m + 128)
            square[lanes, :] = contract(left[:, lanes], right[...], 0)
        lane = lax.broadcasted_iota(jnp.int32, (WIDTH, 128), 1)
        for b in range(3):
            low = slice(128 * b, 128 * b + 128)
            high = slice(HALF + 128 * b, HALF + 128 * b + 128)
            sums, gaps = [], []
            for g in (b, b + 1):
                top = slice(WIDTH * g, WIDTH * g + WIDTH)
                bottom = slice(HALF + WIDTH * g, HALF + WIDTH * g + WIDTH)
                sums.append(square[top, low] + square[bottom, high])
                gaps.append(square[top, high] - square[bottom, low])
            mine = lane < WIDTH - 32 * b
            grads[n, :, low] = jnp.where(mine, sums[0], sums[1]).astype(BF16)
            grads[n + 1, :, low] = jnp.where(mine, gaps[0], gaps[1]).astype(BF16)

    keep_y.wait()
    arrived(1, recv_y)
    lon_forward(recv_y, 1, dual)
    for part in range(2):
        rows = slice(HALF * part, HALF * part + HALF)
        back = contract(dual[...], wide2[rows, :], 1)
        pre[:, rows] = (back * slope[:, rows]).astype(BF16)
    outer(spec, pre, 0)
    outer(act, dual, 2)

    def share(k):
        return grads.at[k // 2, pl.ds(pl.multiple_of(lax.rem(k, 2) * 48, 16), 48), :]

    @pl.loop(1, 8)
    def _(i):
        k = lax.rem(e + i, 8)
        pltpu.make_async_remote_copy(
            src_ref=share(k),
            dst_ref=part1.at[e],
            send_sem=sum_out.at[i],
            recv_sem=sum_in.at[e],
            device_id=(dp, device_of(k, u)),
            device_id_type=MESH,
        ).start()

    for part in range(2):
        rows = slice(HALF * part, HALF * part + HALF)
        store_mixed(contract(pre[...], wide1[rows, :], 1).astype(BF16), part)
    lon_inverse(2, back_y)
    start_all(to_cells, 3, back_y, home_y)
    keep_y = keep_back(back_y, home_y, 3)
    keep_y.start()

    part1[e] = share(e)[...]

    @pl.loop(1, 8)
    def _(i):
        k = lax.rem(e + i, 8)
        pltpu.make_async_remote_copy(
            src_ref=part1.at[k],
            dst_ref=part1.at[k],
            send_sem=sum_out.at[i],
            recv_sem=sum_in.at[k],
            device_id=(dp, device_of(k, u)),
            device_id_type=MESH,
        ).wait_recv()

    total = part1[0].astype(F32)
    for k in range(1, 8):
        total = total + part1[k].astype(F32)
    total = total.astype(BF16)
    for t in range(TILES):
        a, b = t // 3, t % 3
        own1[t] = total[16 * a : 16 * a + 16, 128 * b : 128 * b + 128]

    def reducer(t):
        return (dp_count * t) // TILES

    def to_reducer(t):
        return pltpu.make_async_remote_copy(
            src_ref=own1.at[t],
            dst_ref=part2.at[dp],
            send_sem=dp_out.at[t],
            recv_sem=dp_in.at[dp],
            device_id=(reducer(t), me),
            device_id_type=MESH,
        )

    @pl.loop(0, TILES)
    def _(t):
        @pl.when(dp != reducer(t))
        def _():
            to_reducer(t).start()

    def finish_cells(rows, home, out, n):
        for c in range(3):
            lanes = slice(256 * c, 256 * c + 256)
            got = matmul(lati[...], home[:, :, lanes].reshape(LAT * ROWS, 256))
            got = (got * SCALE).astype(BF16).astype(F32) + rows[:, lanes].astype(F32)
            rows[:, lanes] = got.astype(BF16)
        return pltpu.make_async_copy(rows, out, store_sem.at[n])

    keep_x.wait()
    arrived(2, home_x)
    store_x = finish_cells(xv, home_x, outx_hbm, 0)
    store_x.start()

    mine = ((TILES * dp) + TILES - 1) // dp_count
    reduces = reducer(mine) == dp

    def to_all(i):
        d = lax.rem(dp + i, dp_count)
        return pltpu.make_async_remote_copy(
            src_ref=own3.at[mine],
            dst_ref=own3.at[mine],
            send_sem=cast_out.at[i],
            recv_sem=cast_in.at[mine],
            device_id=(d, me),
            device_id_type=MESH,
        )

    @pl.when(reduces)
    def _():
        part2[dp] = own1[mine]

        @pl.loop(1, dp_count)
        def _(i):
            d = lax.rem(dp + i, dp_count)
            pltpu.make_async_remote_copy(
                src_ref=part2.at[d],
                dst_ref=part2.at[d],
                send_sem=dp_out.at[0],
                recv_sem=dp_in.at[d],
                device_id=(d, me),
                device_id_type=MESH,
            ).wait_recv()

        whole = part2[0].astype(F32)
        for d in range(1, dp_count):
            whole = whole + part2[d].astype(F32)
        own3[mine] = (whole * (1.0 / SAMPLES)).astype(BF16)

        @pl.loop(1, dp_count)
        def _(i):
            to_all(i).start()

    @pl.loop(0, TILES)
    def _(t):
        @pl.when(dp != reducer(t))
        def _():
            pltpu.make_async_remote_copy(
                src_ref=own3.at[t],
                dst_ref=own3.at[t],
                send_sem=cast_out.at[0],
                recv_sem=cast_in.at[t],
                device_id=(reducer(t), me),
                device_id_type=MESH,
            ).wait_recv()

    def to_group(i):
        return pltpu.make_async_remote_copy(
            src_ref=own3,
            dst_ref=final.at[me],
            send_sem=gather_out.at[i],
            recv_sem=gather_in.at[me],
            device_id=(dp, lax.rem(me + i, LON)),
            device_id_type=MESH,
        )

    @pl.loop(1, LON)
    def _(i):
        to_group(i).start()

    final[me] = own3[...]

    keep_y.wait()
    arrived(3, home_y)
    store_y = finish_cells(yv, home_y, outy_hbm, 1)
    store_y.start()

    @pl.loop(1, LON)
    def _(i):
        s = lax.rem(me + i, LON)
        pltpu.make_async_remote_copy(
            src_ref=final.at[s],
            dst_ref=final.at[s],
            send_sem=gather_out.at[i],
            recv_sem=gather_in.at[s],
            device_id=(dp, s),
            device_id_type=MESH,
        ).wait_recv()

    for q in range(4):
        out = (grad1, grad2)[q // 2]
        for v in range(2):
            for t in range(2 * TILES):
                a, b = t // 3, t % 3
                tile = final[4 * q + 2 * v + a // 3, 3 * (a % 3) + b]
                strip[16 * a : 16 * a + 16, 128 * b : 128 * b + 128] = tile.astype(F32)
            for g in range(4):
                out[q % 2, 4 * v + g] = strip[:, WIDTH * g : WIDTH * g + WIDTH]

    stores = [
        pltpu.make_async_copy(grad1, grad1_hbm, store_sem.at[2]),
        pltpu.make_async_copy(grad2, grad2_hbm, store_sem.at[3]),
    ]
    for store in stores:
        store.start()

    @pl.loop(1, LON)
    def _(i):
        to_mixer(0, send_x, recv_x, i).wait_send()
        to_mixer(1, send_y, recv_y, i).wait_send()
        to_cells(2, back_x, home_x, i).wait_send()
        to_cells(3, back_y, home_y, i).wait_send()
        to_group(i).wait_send()

    @pl.loop(1, 8)
    def _(i):
        k = lax.rem(e + i, 8)
        pltpu.make_async_remote_copy(
            src_ref=share(k),
            dst_ref=part1.at[e],
            send_sem=sum_out.at[i],
            recv_sem=sum_in.at[e],
            device_id=(dp, device_of(k, u)),
            device_id_type=MESH,
        ).wait_send()

    @pl.loop(0, TILES)
    def _(t):
        @pl.when(dp != reducer(t))
        def _():
            to_reducer(t).wait_send()

    @pl.when(reduces)
    def _():
        @pl.loop(1, dp_count)
        def _(i):
            to_all(i).wait_send()

    for store in [store_x, store_y, *stores]:
        store.wait()


def on_device(fields, cotangent, first_weight, second_weight):
    dp_count = lax.axis_size("dp")
    rows = ROWS * LAT
    lon = jnp.asarray(lon_matrices(), BF16)
    lat = lat_matrix()
    lat_fwd, lat_inv = jnp.asarray(lat, BF16), jnp.asarray(lat.T.copy(), BF16)
    weight_shape = (2, GROUPS, WIDTH, WIDTH)
    any_spec = pl.BlockSpec(memory_space=pl.ANY)
    dma = pltpu.SemaphoreType.DMA
    cells = pltpu.VMEM((rows, CHANNELS), BF16)
    pairs = pltpu.VMEM((PAIRS, TILE, CHANNELS), BF16)
    lines = pltpu.VMEM((LINES, CHANNELS), BF16)
    blocks = pltpu.VMEM((OWN, LON, TILE, HALF), BF16)
    side = 4 * MODES
    wave, pull, grad1, grad2 = pl.pallas_call(
        kernel,
        out_shape=(
            jax.ShapeDtypeStruct((rows, CHANNELS), BF16),
            jax.ShapeDtypeStruct((rows, CHANNELS), BF16),
            jax.ShapeDtypeStruct(weight_shape, F32),
            jax.ShapeDtypeStruct(weight_shape, F32),
        ),
        in_specs=[any_spec] * 7,
        out_specs=(any_spec,) * 4,
        scratch_shapes=[
            cells, cells,
            pltpu.VMEM(weight_shape, BF16), pltpu.VMEM(weight_shape, BF16),
            pltpu.VMEM((8, side, side), BF16),
            pltpu.VMEM((rows, rows), BF16), pltpu.VMEM((rows, rows), BF16),
            pairs, pairs, blocks, blocks, blocks, blocks, pairs, pairs,
            pltpu.VMEM((CHANNELS, CHANNELS), BF16), pltpu.VMEM((CHANNELS, CHANNELS), BF16),
            pltpu.VMEM((2, HALF, HALF), F32),
            lines, lines, lines, lines,
            pltpu.VMEM((LINES, CHANNELS), F32),
            pltpu.VMEM((OWN, side, HALF), BF16),
            pltpu.VMEM((CHANNELS, CHANNELS), F32),
            pltpu.VMEM((4, WIDTH, HALF), BF16),
            pltpu.VMEM((8, 48, HALF), BF16),
            pltpu.VMEM((TILES, 16, 128), BF16),
            pltpu.VMEM((dp_count, 16, 128), BF16),
            pltpu.VMEM((TILES, 16, 128), BF16),
            pltpu.VMEM((LON, TILES, 16, 128), BF16),
            pltpu.VMEM((WIDTH, HALF), F32),
            pltpu.VMEM(weight_shape, F32), pltpu.VMEM(weight_shape, F32),
            dma((8,)), dma((4,)), dma((4,)), dma((4, LON)), dma((4, LON)),
            dma((8,)), dma((8,)), dma((TILES,)), dma((dp_count,)),
            dma((dp_count,)), dma((TILES,)), dma((LON,)), dma((LON,)),
        ],
        compiler_params=pltpu.CompilerParams(
            collective_id=0, has_side_effects=True, vmem_limit_bytes=48 << 20
        ),
    )(
        fields.reshape(rows, CHANNELS), cotangent.reshape(rows, CHANNELS),
        first_weight, second_weight, lon, lat_fwd, lat_inv,
    )
    shape = (1, ROWS, LAT, CHANNELS)
    return wave.reshape(shape), pull.reshape(shape), grad1, grad2


def solution(mesh):
    placed = (P("dp", "lon", None, None), P("dp", "lon", None, None), P(), P())
    return jax.shard_map(
        on_device, mesh=mesh, in_specs=placed, out_specs=placed, check_vma=False
    )
```

```python
import math

import jax
import jax.numpy as jnp
import ml_dtypes
import numpy as np
from jax import lax
from jax.experimental import pallas as pl
from jax.experimental.pallas import tpu as pltpu
from jax.sharding import PartitionSpec as P

COEF = 0.7978845608028654
CUBIC = 0.044715

SAMPLES = 32
CELLS = 128
LAT = 48
MODES = 64
CHANNELS = 768
GROUPS = 8
WIDTH = 96

LON = 16
ROWS = CELLS // LON
HALF = CHANNELS // 2
PAIRS = LAT // 2
OWN = PAIRS // (LON // 2)
TILE = 2 * ROWS
LINES = OWN * 2 * MODES
TILES = 9
SCALE = 1.0 / math.sqrt(CELLS * LAT)
MESH = pl.DeviceIdType.MESH
BF16 = jnp.bfloat16
F32 = jnp.float32


def make_basis(length, count):
    product = np.arange(length)[:, None] * np.arange(count)[None, :] % length
    angle = product.astype(np.float32) * np.float32(2.0 * math.pi / length)
    table = np.stack([np.cos(angle), -np.sin(angle)], axis=-1)
    return table.astype(ml_dtypes.bfloat16).astype(np.float32)


def lat_matrix():
    table = make_basis(LAT, LAT)
    half = np.zeros((PAIRS, 2, LAT), np.float32)
    half[0, 0] = table[:, 0, 0]
    half[0, 1] = table[:, PAIRS, 0]
    for j in range(1, PAIRS):
        half[j, 0] = table[:, j, 0]
        half[j, 1] = table[:, j, 1]
    full = np.einsum("pah,wv->pawvh", half, np.eye(ROWS, dtype=np.float32))
    return full.reshape(PAIRS * 2 * ROWS, ROWS * LAT)


def lon_matrix(special, weighted):
    table = make_basis(CELLS, MODES)
    cos, sin = table[:, :, 0].T, table[:, :, 1].T
    if weighted:
        factor = np.where(np.arange(MODES) == 0, 1.0, 2.0).astype(np.float32)[:, None]
        cos, sin = cos * factor, sin * factor
    zero = np.zeros_like(cos)
    if special:
        from_real = [cos, sin, zero, zero]
        from_imag = [zero, zero, cos, sin]
    else:
        from_real = [cos, sin, cos, sin]
        from_imag = [-sin, cos, sin, -cos]
    both = np.stack([np.concatenate(from_real), np.concatenate(from_imag)], axis=1)
    both = both.reshape(4 * MODES, 2, LON, ROWS).transpose(0, 2, 1, 3)
    return both.reshape(4 * MODES, 2 * CELLS)


def lon_matrices():
    found = []
    for special in (False, True):
        plain, weighted = lon_matrix(special, False), lon_matrix(special, True)
        found += [plain, weighted, plain.T, weighted.T]
    return np.stack(found)


def matmul(left, right):
    return jnp.dot(left, right, preferred_element_type=F32)


def contract(left, right, axis):
    return lax.dot_general(
        left, right, (((axis,), (axis,)), ((), ())), preferred_element_type=F32
    )


def kernel(
    x_hbm, y_hbm, w1_hbm, w2_hbm, lon_hbm, latf_hbm, lati_hbm,
    outx_hbm, outy_hbm, grad1_hbm, grad2_hbm,
    xv, yv, w1v, w2v, lonv, latf, lati,
    send_x, send_y, recv_x, recv_y, back_x, back_y, home_x, home_y,
    wide1, wide2, place, spec, dual, act, pre, slope, mixed,
    square, grads, part1, own1, part2, own3, final, strip, grad1, grad2,
    load_sem, store_sem, self_sem, out_sem, in_sem,
    sum_out, sum_in, dp_out, dp_in, cast_out, cast_in, gather_out, gather_in,
):
    dp_count = lax.axis_size("dp")
    me, dp = lax.axis_index("lon"), lax.axis_index("dp")

    def half_of(s):
        return lax.rem(s // 2, 2)

    def slot_of(s):
        return (s // 4) * 2 + lax.rem(s, 2)

    def device_of(e, u):
        return (e // 2) * 4 + u * 2 + lax.rem(e, 2)

    u, e = half_of(me), slot_of(me)
    first = jnp.where(e == 0, 4, 0)

    loads = [
        pltpu.make_async_copy(x_hbm, xv, load_sem.at[0]),
        pltpu.make_async_copy(latf_hbm, latf, load_sem.at[1]),
        pltpu.make_async_copy(y_hbm, yv, load_sem.at[2]),
        pltpu.make_async_copy(w1_hbm, w1v, load_sem.at[3]),
        pltpu.make_async_copy(w2_hbm, w2v, load_sem.at[4]),
        pltpu.make_async_copy(lon_hbm.at[pl.ds(0, 4)], lonv.at[pl.ds(0, 4)], load_sem.at[5]),
        pltpu.make_async_copy(lon_hbm.at[pl.ds(first, 4)], lonv.at[pl.ds(4, 4)], load_sem.at[6]),
        pltpu.make_async_copy(lati_hbm, lati, load_sem.at[7]),
    ]
    for load in loads:
        load.start()

    barrier = pltpu.get_barrier_semaphore()

    @pl.loop(1, LON)
    def _(i):
        pl.semaphore_signal(
            barrier, inc=1, device_id=(dp, lax.rem(me + i, LON)), device_id_type=MESH
        )

    @pl.loop(1, dp_count)
    def _(i):
        pl.semaphore_signal(
            barrier, inc=1, device_id=(lax.rem(dp + i, dp_count), me), device_id_type=MESH
        )

    def lat_forward(rows, out):
        for n in range(3):
            lanes = slice(256 * n, 256 * n + 256)
            got = matmul(latf[...], rows[:, lanes]).astype(BF16)
            out[:, :, lanes] = got.reshape(PAIRS, TILE, 256)

    def block_of(buf, s):
        lanes = pl.ds(pl.multiple_of(half_of(s) * HALF, 128), HALF)
        return buf.at[pl.ds(slot_of(s) * OWN, OWN), :, lanes]

    def to_mixer(stage, src, dst, i):
        s = lax.rem(me + i, LON)
        return pltpu.make_async_remote_copy(
            src_ref=block_of(src, s),
            dst_ref=dst.at[:, me],
            send_sem=out_sem.at[stage, i],
            recv_sem=in_sem.at[stage, me],
            device_id=(dp, s),
            device_id_type=MESH,
        )

    def to_cells(stage, src, dst, i):
        s = lax.rem(me + i, LON)
        return pltpu.make_async_remote_copy(
            src_ref=src.at[:, s],
            dst_ref=block_of(dst, me),
            send_sem=out_sem.at[stage, i],
            recv_sem=in_sem.at[stage, me],
            device_id=(dp, s),
            device_id_type=MESH,
        )

    def start_all(make, stage, src, dst):
        @pl.loop(1, LON)
        def _(i):
            make(stage, src, dst, LON - i).start()

    def arrived(stage, buf):
        @pl.loop(1, LON)
        def _(i):
            s = lax.rem(me + i, LON)
            if stage < 2:
                spot = buf.at[:, s]
            else:
                spot = block_of(buf, s)
            pltpu.make_async_remote_copy(
                src_ref=spot,
                dst_ref=spot,
                send_sem=out_sem.at[stage, i],
                recv_sem=in_sem.at[stage, s],
                device_id=(dp, s),
                device_id_type=MESH,
            ).wait_recv()

    def keep_forward(src, dst, n):
        return pltpu.make_async_copy(block_of(src, me), dst.at[:, me], self_sem.at[n])

    def keep_back(src, dst, n):
        return pltpu.make_async_copy(src.at[:, me], block_of(dst, me), self_sem.at[n])

    loads[0].wait()
    loads[1].wait()
    lat_forward(xv, send_x)
    pl.semaphore_wait(barrier, LON - 1 + dp_count - 1)
    start_all(to_mixer, 0, send_x, recv_x)
    keep_x = keep_forward(send_x, recv_x, 0)
    keep_x.start()
    loads[2].wait()
    lat_forward(yv, send_y)
    start_all(to_mixer, 1, send_y, recv_y)
    keep_y = keep_forward(send_y, recv_y, 1)
    keep_y.start()

    def widen(weight, wide):
        for p in range(2):
            for g in range(4):
                own = slice(WIDTH * g, WIDTH * g + WIDTH)
                place[p, own, own] = weight[p, 4 * u + g].astype(F32)
        real, imag = place[0].astype(BF16), place[1].astype(BF16)
        wide[:HALF, :HALF] = real
        wide[HALF:, HALF:] = real
        wide[:HALF, HALF:] = imag
        wide[HALF:, :HALF] = -imag

    place[...] = jnp.zeros_like(place)
    for load in loads[3:]:
        load.wait()
    widen(w1v, wide1)
    widen(w2v, wide2)

    def lon_forward(buf, kind, out):
        for p in range(OWN):
            table = lonv[kind + (4 if p == 0 else 0)]
            got = matmul(table, buf[p].reshape(2 * CELLS, HALF))
            got = (got * SCALE).astype(BF16)
            for x in range(2):
                rows = slice((2 * p + x) * MODES, (2 * p + x + 1) * MODES)
                out[rows, :HALF] = got[2 * x * MODES : (2 * x + 1) * MODES]
                out[rows, HALF:] = got[(2 * x + 1) * MODES : (2 * x + 2) * MODES]

    def store_mixed(got, part):
        for p in range(OWN):
            for x in range(2):
                rows = slice((2 * p + x) * MODES, (2 * p + x + 1) * MODES)
                to = slice((2 * x + part) * MODES, (2 * x + part + 1) * MODES)
                mixed[p, to, :] = got[rows]

    def lon_inverse(kind, out):
        for p in range(OWN):
            table = lonv[kind + (4 if p == 0 else 0)]
            got = matmul(table, mixed[p]).astype(BF16)
            out[p] = got.reshape(LON, TILE, HALF)

    keep_x.wait()
    arrived(0, recv_x)
    lon_forward(recv_x, 0, spec)
    for part in range(2):
        lanes = slice(HALF * part, HALF * part + HALF)
        inner = matmul(spec[...], wide1[:, lanes])
        hyper = jnp.tanh(COEF * (inner + CUBIC * inner * inner * inner))
        act[:, lanes] = (0.5 * inner * (1.0 + hyper)).astype(BF16)
        slope[:, lanes] = 0.5 * (1.0 + hyper) + 0.5 * inner * (1.0 - hyper * hyper) * COEF * (
            1.0 + 3.0 * CUBIC * inner * inner
        )
    for part in range(2):
        lanes = slice(HALF * part, HALF * part + HALF)
        store_mixed(matmul(act[...], wide2[:, lanes]).astype(BF16), part)
    lon_inverse(3, back_x)

    def outer(left, right, n):
        for m in range(6):
            lanes = slice(128 * m, 128 * m + 128)
            square[lanes, :] = contract(left[:, lanes], right[...], 0)
        lane = lax.broadcasted_iota(jnp.int32, (WIDTH, 128), 1)
        for b in range(3):
            low = slice(128 * b, 128 * b + 128)
            high = slice(HALF + 128 * b, HALF + 128 * b + 128)
            sums, gaps = [], []
            for g in (b, b + 1):
                top = slice(WIDTH * g, WIDTH * g + WIDTH)
                bottom = slice(HALF + WIDTH * g, HALF + WIDTH * g + WIDTH)
                sums.append(square[top, low] + square[bottom, high])
                gaps.append(square[top, high] - square[bottom, low])
            mine = lane < WIDTH - 32 * b
            grads[n, :, low] = jnp.where(mine, sums[0], sums[1]).astype(BF16)
            grads[n + 1, :, low] = jnp.where(mine, gaps[0], gaps[1]).astype(BF16)

    keep_y.wait()
    arrived(1, recv_y)
    lon_forward(recv_y, 1, dual)
    for part in range(2):
        rows = slice(HALF * part, HALF * part + HALF)
        back = contract(dual[...], wide2[rows, :], 1)
        pre[:, rows] = (back * slope[:, rows]).astype(BF16)
    outer(spec, pre, 0)
    outer(act, dual, 2)

    def share(k):
        return grads.at[k // 2, pl.ds(pl.multiple_of(lax.rem(k, 2) * 48, 16), 48), :]

    def to_owner(i):
        k = lax.rem(e + i, 8)
        return pltpu.make_async_remote_copy(
            src_ref=share(k),
            dst_ref=part1.at[e],
            send_sem=sum_out.at[i],
            recv_sem=sum_in.at[e],
            device_id=(dp, device_of(k, u)),
            device_id_type=MESH,
        )

    def send_shares():
        @pl.loop(1, 8)
        def _(i):
            to_owner(i).start()

    send_shares()

    for part in range(2):
        rows = slice(HALF * part, HALF * part + HALF)
        store_mixed(contract(pre[...], wide1[rows, :], 1).astype(BF16), part)
    lon_inverse(2, back_y)

    def sum_shares():
        part1[e] = share(e)[...]

        @pl.loop(1, 8)
        def _(i):
            k = lax.rem(e + i, 8)
            pltpu.make_async_remote_copy(
                src_ref=part1.at[k],
                dst_ref=part1.at[k],
                send_sem=sum_out.at[i],
                recv_sem=sum_in.at[k],
                device_id=(dp, device_of(k, u)),
                device_id_type=MESH,
            ).wait_recv()

        total = part1[0].astype(F32)
        for k in range(1, 8):
            total = total + part1[k].astype(F32)
        total = total.astype(BF16)
        for t in range(TILES):
            a, b = t // 3, t % 3
            own1[t] = total[16 * a : 16 * a + 16, 128 * b : 128 * b + 128]

    sum_shares()

    def reducer(t):
        return (dp_count * t) // TILES

    def to_reducer(t):
        return pltpu.make_async_remote_copy(
            src_ref=own1.at[t],
            dst_ref=part2.at[dp],
            send_sem=dp_out.at[t],
            recv_sem=dp_in.at[dp],
            device_id=(reducer(t), me),
            device_id_type=MESH,
        )

    def send_tiles():
        @pl.loop(0, TILES)
        def _(t):
            @pl.when(dp != reducer(t))
            def _():
                to_reducer(t).start()

    send_tiles()
    start_all(to_cells, 2, back_x, home_x)
    keep_x = keep_back(back_x, home_x, 2)
    keep_x.start()
    start_all(to_cells, 3, back_y, home_y)
    keep_y = keep_back(back_y, home_y, 3)
    keep_y.start()

    def finish_cells(rows, home, out, n):
        for c in range(3):
            lanes = slice(256 * c, 256 * c + 256)
            got = matmul(lati[...], home[:, :, lanes].reshape(LAT * ROWS, 256))
            got = (got * SCALE).astype(BF16).astype(F32) + rows[:, lanes].astype(F32)
            rows[:, lanes] = got.astype(BF16)
        return pltpu.make_async_copy(rows, out, store_sem.at[n])


    mine = ((TILES * dp) + TILES - 1) // dp_count
    reduces = reducer(mine) == dp

    def to_all(i):
        d = lax.rem(dp + i, dp_count)
        return pltpu.make_async_remote_copy(
            src_ref=own3.at[mine],
            dst_ref=own3.at[mine],
            send_sem=cast_out.at[i],
            recv_sem=cast_in.at[mine],
            device_id=(d, me),
            device_id_type=MESH,
        )

    @pl.when(reduces)
    def _():
        part2[dp] = own1[mine]

        @pl.loop(1, dp_count)
        def _(i):
            d = lax.rem(dp + i, dp_count)
            pltpu.make_async_remote_copy(
                src_ref=part2.at[d],
                dst_ref=part2.at[d],
                send_sem=dp_out.at[0],
                recv_sem=dp_in.at[d],
                device_id=(d, me),
                device_id_type=MESH,
            ).wait_recv()

        whole = part2[0].astype(F32)
        for d in range(1, dp_count):
            whole = whole + part2[d].astype(F32)
        own3[mine] = (whole * (1.0 / SAMPLES)).astype(BF16)

        @pl.loop(1, dp_count)
        def _(i):
            to_all(i).start()

    keep_x.wait()
    arrived(2, home_x)
    store_x = finish_cells(xv, home_x, outx_hbm, 0)
    store_x.start()

    keep_y.wait()
    arrived(3, home_y)
    store_y = finish_cells(yv, home_y, outy_hbm, 1)
    store_y.start()

    @pl.loop(0, TILES)
    def _(t):
        @pl.when(dp != reducer(t))
        def _():
            pltpu.make_async_remote_copy(
                src_ref=own3.at[t],
                dst_ref=own3.at[t],
                send_sem=cast_out.at[0],
                recv_sem=cast_in.at[t],
                device_id=(reducer(t), me),
                device_id_type=MESH,
            ).wait_recv()

    twin = me + 1 - 2 * lax.rem(me, 2)

    def to_chips(i):
        return pltpu.make_async_remote_copy(
            src_ref=own3,
            dst_ref=final.at[me],
            send_sem=gather_out.at[i],
            recv_sem=gather_in.at[me],
            device_id=(dp, lax.rem(me + 2 * i, LON)),
            device_id_type=MESH,
        )

    def to_twin(i):
        s = lax.rem(me + 2 * i, LON)
        return pltpu.make_async_remote_copy(
            src_ref=final.at[s],
            dst_ref=final.at[s],
            send_sem=gather_out.at[8 + i],
            recv_sem=gather_in.at[s],
            device_id=(dp, twin),
            device_id_type=MESH,
        )

    def from_peer(s, sender):
        return pltpu.make_async_remote_copy(
            src_ref=final.at[s],
            dst_ref=final.at[s],
            send_sem=gather_out.at[0],
            recv_sem=gather_in.at[s],
            device_id=(dp, sender),
            device_id_type=MESH,
        )

    def gather_start():
        @pl.loop(1, 8)
        def _(i):
            to_chips(8 - i).start()

        final[me] = own3[...]
        to_twin(0).start()

    def gather_forward():
        @pl.loop(1, 8)
        def _(i):
            s = lax.rem(me + 2 * i, LON)
            from_peer(s, s).wait_recv()
            to_twin(i).start()

    def gather_wait():
        @pl.loop(0, 8)
        def _(i):
            from_peer(lax.rem(twin + 2 * i, LON), twin).wait_recv()

    def gather_sent():
        @pl.loop(1, 8)
        def _(i):
            to_chips(i).wait_send()
            to_twin(i).wait_send()

        to_twin(0).wait_send()

    gather_start()

    gather_forward()

    gather_wait()

    def unpack():
        for q in range(4):
            out = (grad1, grad2)[q // 2]
            for v in range(2):
                for t in range(2 * TILES):
                    a, b = t // 3, t % 3
                    tile = final[4 * q + 2 * v + a // 3, 3 * (a % 3) + b]
                    strip[16 * a : 16 * a + 16, 128 * b : 128 * b + 128] = tile.astype(F32)
                for g in range(4):
                    out[q % 2, 4 * v + g] = strip[:, WIDTH * g : WIDTH * g + WIDTH]

    unpack()

    stores = [
        pltpu.make_async_copy(grad1, grad1_hbm, store_sem.at[2]),
        pltpu.make_async_copy(grad2, grad2_hbm, store_sem.at[3]),
    ]
    for store in stores:
        store.start()

    @pl.loop(1, LON)
    def _(i):
        to_mixer(0, send_x, recv_x, i).wait_send()
        to_mixer(1, send_y, recv_y, i).wait_send()
        to_cells(2, back_x, home_x, i).wait_send()
        to_cells(3, back_y, home_y, i).wait_send()

    def shares_sent():
        @pl.loop(1, 8)
        def _(i):
            to_owner(i).wait_send()

    shares_sent()
    gather_sent()

    @pl.loop(0, TILES)
    def _(t):
        @pl.when(dp != reducer(t))
        def _():
            to_reducer(t).wait_send()

    @pl.when(reduces)
    def _():
        @pl.loop(1, dp_count)
        def _(i):
            to_all(i).wait_send()

    for store in [store_x, store_y, *stores]:
        store.wait()


def on_device(fields, cotangent, first_weight, second_weight):
    dp_count = lax.axis_size("dp")
    rows = ROWS * LAT
    lon = jnp.asarray(lon_matrices(), BF16)
    lat = lat_matrix()
    lat_fwd, lat_inv = jnp.asarray(lat, BF16), jnp.asarray(lat.T.copy(), BF16)
    weight_shape = (2, GROUPS, WIDTH, WIDTH)
    any_spec = pl.BlockSpec(memory_space=pl.ANY)
    dma = pltpu.SemaphoreType.DMA
    cells = pltpu.VMEM((rows, CHANNELS), BF16)
    pairs = pltpu.VMEM((PAIRS, TILE, CHANNELS), BF16)
    lines = pltpu.VMEM((LINES, CHANNELS), BF16)
    blocks = pltpu.VMEM((OWN, LON, TILE, HALF), BF16)
    side = 4 * MODES
    wave, pull, grad1, grad2 = pl.pallas_call(
        kernel,
        out_shape=(
            jax.ShapeDtypeStruct((rows, CHANNELS), BF16),
            jax.ShapeDtypeStruct((rows, CHANNELS), BF16),
            jax.ShapeDtypeStruct(weight_shape, F32),
            jax.ShapeDtypeStruct(weight_shape, F32),
        ),
        in_specs=[any_spec] * 7,
        out_specs=(any_spec,) * 4,
        scratch_shapes=[
            cells, cells,
            pltpu.VMEM(weight_shape, BF16), pltpu.VMEM(weight_shape, BF16),
            pltpu.VMEM((8, side, side), BF16),
            pltpu.VMEM((rows, rows), BF16), pltpu.VMEM((rows, rows), BF16),
            pairs, pairs, blocks, blocks, blocks, blocks, pairs, pairs,
            pltpu.VMEM((CHANNELS, CHANNELS), BF16), pltpu.VMEM((CHANNELS, CHANNELS), BF16),
            pltpu.VMEM((2, HALF, HALF), F32),
            lines, lines, lines, lines,
            pltpu.VMEM((LINES, CHANNELS), F32),
            pltpu.VMEM((OWN, side, HALF), BF16),
            pltpu.VMEM((CHANNELS, CHANNELS), F32),
            pltpu.VMEM((4, WIDTH, HALF), BF16),
            pltpu.VMEM((8, 48, HALF), BF16),
            pltpu.VMEM((TILES, 16, 128), BF16),
            pltpu.VMEM((dp_count, 16, 128), BF16),
            pltpu.VMEM((TILES, 16, 128), BF16),
            pltpu.VMEM((LON, TILES, 16, 128), BF16),
            pltpu.VMEM((WIDTH, HALF), F32),
            pltpu.VMEM(weight_shape, F32), pltpu.VMEM(weight_shape, F32),
            dma((8,)), dma((4,)), dma((4,)), dma((4, LON)), dma((4, LON)),
            dma((8,)), dma((8,)), dma((TILES,)), dma((dp_count,)),
            dma((dp_count,)), dma((TILES,)), dma((LON,)), dma((LON,)),
        ],
        compiler_params=pltpu.CompilerParams(
            collective_id=0, has_side_effects=True, vmem_limit_bytes=63 << 20
        ),
    )(
        fields.reshape(rows, CHANNELS), cotangent.reshape(rows, CHANNELS),
        first_weight, second_weight, lon, lat_fwd, lat_inv,
    )
    shape = (1, ROWS, LAT, CHANNELS)
    return wave.reshape(shape), pull.reshape(shape), grad1, grad2


def solution(mesh):
    placed = (P("dp", "lon", None, None), P("dp", "lon", None, None), P(), P())
    return jax.shard_map(
        on_device, mesh=mesh, in_specs=placed, out_specs=placed, check_vma=False
    )
```

```python
import math

import jax
import jax.numpy as jnp
import ml_dtypes
import numpy as np
from jax import lax
from jax.experimental import pallas as pl
from jax.experimental.pallas import tpu as pltpu
from jax.sharding import PartitionSpec as P

COEF = 0.7978845608028654
CUBIC = 0.044715

SAMPLES = 32
CELLS = 128
LAT = 48
MODES = 64
CHANNELS = 768
GROUPS = 8
WIDTH = 96

LON = 16
ROWS = CELLS // LON
HALF = CHANNELS // 2
PAIRS = LAT // 2
OWN = PAIRS // (LON // 2)
TILE = 2 * ROWS
LINES = OWN * 2 * MODES
TILES = 9
SCALE = 1.0 / math.sqrt(CELLS * LAT)
MESH = pl.DeviceIdType.MESH
BF16 = jnp.bfloat16
F32 = jnp.float32


def make_basis(length, count):
    product = np.arange(length)[:, None] * np.arange(count)[None, :] % length
    angle = product.astype(np.float32) * np.float32(2.0 * math.pi / length)
    table = np.stack([np.cos(angle), -np.sin(angle)], axis=-1)
    return table.astype(ml_dtypes.bfloat16).astype(np.float32)


def lat_matrix():
    table = make_basis(LAT, LAT)
    half = np.zeros((PAIRS, 2, LAT), np.float32)
    half[0, 0] = table[:, 0, 0]
    half[0, 1] = table[:, PAIRS, 0]
    for j in range(1, PAIRS):
        half[j, 0] = table[:, j, 0]
        half[j, 1] = table[:, j, 1]
    full = np.einsum("pah,wv->pawvh", half, np.eye(ROWS, dtype=np.float32))
    return full.reshape(PAIRS * 2 * ROWS, ROWS * LAT)


def lon_matrix(special, weighted):
    table = make_basis(CELLS, MODES)
    cos, sin = table[:, :, 0].T, table[:, :, 1].T
    if weighted:
        factor = np.where(np.arange(MODES) == 0, 1.0, 2.0).astype(np.float32)[:, None]
        cos, sin = cos * factor, sin * factor
    zero = np.zeros_like(cos)
    if special:
        from_real = [cos, sin, zero, zero]
        from_imag = [zero, zero, cos, sin]
    else:
        from_real = [cos, sin, cos, sin]
        from_imag = [-sin, cos, sin, -cos]
    both = np.stack([np.concatenate(from_real), np.concatenate(from_imag)], axis=1)
    both = both.reshape(4 * MODES, 2, LON, ROWS).transpose(0, 2, 1, 3)
    return both.reshape(4 * MODES, 2 * CELLS)


def lon_matrices():
    found = []
    for special in (False, True):
        plain, weighted = lon_matrix(special, False), lon_matrix(special, True)
        found += [plain, weighted, plain.T, weighted.T]
    return np.stack(found)


def matmul(left, right):
    return jnp.dot(left, right, preferred_element_type=F32)


def kernel(
    x_hbm, y_hbm, w1_hbm, w2_hbm, lon_hbm, latf_hbm, lati_hbm,
    outx_hbm, outy_hbm, grads_hbm,
    xv, yv, w1v, w2v, lonv, latf, lati,
    send_x, send_y, recv_x, recv_y, back_x, back_y, home_x, home_y,
    wide1, wide2, turned1, turned2, place, spec, dual, act, pre, slope, mixed,
    spec_t, act_t, grads, part1, own1, part2, own3, final,
    load_sem, store_sem, self_sem, out_sem, in_sem,
    sum_out, sum_in, dp_out, dp_in, cast_out, cast_in, gather_out, gather_in, relay,
):
    dp_count = lax.axis_size("dp")
    me, dp = lax.axis_index("lon"), lax.axis_index("dp")
    ring, z, side = dp_count // 2, dp // 2, lax.rem(dp, 2)

    def half_of(s):
        return lax.rem(s // 2, 2)

    def slot_of(s):
        return (s // 4) * 2 + lax.rem(s, 2)

    def device_of(e, u):
        return (e // 2) * 4 + u * 2 + lax.rem(e, 2)

    u, e = half_of(me), slot_of(me)
    first = jnp.where(e == 0, 4, 0)

    loads = [
        pltpu.make_async_copy(x_hbm, xv, load_sem.at[0]),
        pltpu.make_async_copy(latf_hbm, latf, load_sem.at[1]),
        pltpu.make_async_copy(y_hbm, yv, load_sem.at[2]),
        pltpu.make_async_copy(w1_hbm, w1v, load_sem.at[3]),
        pltpu.make_async_copy(w2_hbm, w2v, load_sem.at[4]),
        pltpu.make_async_copy(lon_hbm.at[pl.ds(0, 4)], lonv.at[pl.ds(0, 4)], load_sem.at[5]),
        pltpu.make_async_copy(lon_hbm.at[pl.ds(first, 4)], lonv.at[pl.ds(4, 4)], load_sem.at[6]),
        pltpu.make_async_copy(lati_hbm, lati, load_sem.at[7]),
    ]
    barrier = pltpu.get_barrier_semaphore()

    @pl.loop(1, LON)
    def _(i):
        pl.semaphore_signal(
            barrier, inc=1, device_id=(dp, lax.rem(me + i, LON)), device_id_type=MESH
        )

    def along(step):
        return lax.rem(z + step + ring, ring) * 2 + side

    turn = 1 - 2 * side
    for other in (along(1), along(-1), dp + turn, along(1) + turn, along(-1) + turn):
        pl.semaphore_signal(barrier, inc=1, device_id=(other, me), device_id_type=MESH)

    for load in loads:
        load.start()

    def announce(r):
        for step in (2**r, -(2**r)):
            pl.semaphore_signal(
                relay.at[r], inc=1, device_id=(along(step), me), device_id_type=MESH
            )

    def heard(r):
        pl.semaphore_wait(relay.at[r], 2)

    def lat_forward(rows, out):
        for n in range(3):
            lanes = slice(256 * n, 256 * n + 256)
            got = matmul(latf[...], rows[:, lanes]).astype(BF16)
            out[:, :, lanes] = got.reshape(PAIRS, TILE, 256)

    def block_of(buf, s):
        lanes = pl.ds(pl.multiple_of(half_of(s) * HALF, 128), HALF)
        return buf.at[pl.ds(slot_of(s) * OWN, OWN), :, lanes]

    def to_mixer(stage, src, dst, i):
        s = lax.rem(me + i, LON)
        return pltpu.make_async_remote_copy(
            src_ref=block_of(src, s),
            dst_ref=dst.at[:, me],
            send_sem=out_sem.at[stage, i],
            recv_sem=in_sem.at[stage, me],
            device_id=(dp, s),
            device_id_type=MESH,
        )

    def to_cells(stage, src, dst, i):
        s = lax.rem(me + i, LON)
        return pltpu.make_async_remote_copy(
            src_ref=src.at[:, s],
            dst_ref=block_of(dst, me),
            send_sem=out_sem.at[stage, i],
            recv_sem=in_sem.at[stage, me],
            device_id=(dp, s),
            device_id_type=MESH,
        )

    def start_all(make, stage, src, dst):
        @pl.loop(1, LON)
        def _(i):
            make(stage, src, dst, LON - i).start()

    def arrived(stage, buf):
        @pl.loop(1, LON)
        def _(i):
            s = lax.rem(me + i, LON)
            if stage < 2:
                spot = buf.at[:, s]
            else:
                spot = block_of(buf, s)
            pltpu.make_async_remote_copy(
                src_ref=spot,
                dst_ref=spot,
                send_sem=out_sem.at[stage, i],
                recv_sem=in_sem.at[stage, s],
                device_id=(dp, s),
                device_id_type=MESH,
            ).wait_recv()

    def keep_forward(src, dst, n):
        return pltpu.make_async_copy(block_of(src, me), dst.at[:, me], self_sem.at[n])

    def keep_back(src, dst, n):
        return pltpu.make_async_copy(src.at[:, me], block_of(dst, me), self_sem.at[n])

    loads[0].wait()
    loads[1].wait()
    lat_forward(xv, send_x)
    pl.semaphore_wait(barrier, LON - 1 + 5)
    start_all(to_mixer, 0, send_x, recv_x)
    keep_x = keep_forward(send_x, recv_x, 0)
    keep_x.start()
    loads[2].wait()
    lat_forward(yv, send_y)
    start_all(to_mixer, 1, send_y, recv_y)
    keep_y = keep_forward(send_y, recv_y, 1)
    keep_y.start()
    announce(0)

    def widen(weight, wide, turned):
        for p in range(2):
            for g in range(4):
                own = slice(WIDTH * g, WIDTH * g + WIDTH)
                place[p, own, own] = weight[p, 4 * u + g].astype(F32)
        real, imag = place[0].astype(BF16), place[1].astype(BF16)
        wide[:HALF, :HALF] = real
        wide[HALF:, HALF:] = real
        wide[:HALF, HALF:] = imag
        wide[HALF:, :HALF] = -imag
        real, imag = place[0].T.astype(BF16), place[1].T.astype(BF16)
        turned[:HALF, :HALF] = real
        turned[HALF:, HALF:] = real
        turned[:HALF, HALF:] = -imag
        turned[HALF:, :HALF] = imag

    place[...] = jnp.zeros_like(place)
    for load in loads[3:]:
        load.wait()
    widen(w1v, wide1, turned1)
    widen(w2v, wide2, turned2)
    heard(0)
    announce(1)

    def lon_forward(buf, kind, out):
        for p in range(OWN):
            table = lonv[kind + (4 if p == 0 else 0)]
            got = matmul(table, buf[p].reshape(2 * CELLS, HALF))
            got = (got * SCALE).astype(BF16)
            for x in range(2):
                rows = slice((2 * p + x) * MODES, (2 * p + x + 1) * MODES)
                out[rows, :HALF] = got[2 * x * MODES : (2 * x + 1) * MODES]
                out[rows, HALF:] = got[(2 * x + 1) * MODES : (2 * x + 2) * MODES]

    def store_mixed(got, part):
        for p in range(OWN):
            for x in range(2):
                rows = slice((2 * p + x) * MODES, (2 * p + x + 1) * MODES)
                to = slice((2 * x + part) * MODES, (2 * x + part + 1) * MODES)
                mixed[p, to, :] = got[rows]

    def lon_inverse(kind, out):
        for p in range(OWN):
            table = lonv[kind + (4 if p == 0 else 0)]
            got = matmul(table, mixed[p]).astype(BF16)
            out[p] = got.reshape(LON, TILE, HALF)

    keep_x.wait()
    arrived(0, recv_x)
    lon_forward(recv_x, 0, spec)
    for part in range(2):
        lanes = slice(HALF * part, HALF * part + HALF)
        inner = matmul(spec[...], wide1[:, lanes])
        hyper = jnp.tanh(COEF * (inner + CUBIC * inner * inner * inner))
        act[:, lanes] = (0.5 * inner * (1.0 + hyper)).astype(BF16)
        slope[:, lanes] = 0.5 * (1.0 + hyper) + 0.5 * inner * (1.0 - hyper * hyper) * COEF * (
            1.0 + 3.0 * CUBIC * inner * inner
        )
    for part in range(2):
        lanes = slice(HALF * part, HALF * part + HALF)
        store_mixed(matmul(act[...], wide2[:, lanes]).astype(BF16), part)
    lon_inverse(3, back_x)

    heard(1)
    announce(2)

    spec_t[...] = spec[...].T
    act_t[...] = act[...].T

    def outer(left_t, right, n):
        lane = lax.broadcasted_iota(jnp.int32, (WIDTH, 128), 1)
        for b in range(3):
            low = slice(128 * b, 128 * b + 128)
            high = slice(HALF + 128 * b, HALF + 128 * b + 128)
            columns = jnp.concatenate([right[:, low], right[:, high]], axis=1)
            span = 2 * WIDTH
            top = matmul(left_t[WIDTH * b : WIDTH * b + span, :], columns)
            bottom = matmul(left_t[HALF + WIDTH * b : HALF + WIDTH * b + span, :], columns)
            sums = top[:, :128] + bottom[:, 128:]
            gaps = top[:, 128:] - bottom[:, :128]
            mine = lane < WIDTH - 32 * b
            grads[n, :, low] = jnp.where(mine, sums[:WIDTH], sums[WIDTH:]).astype(BF16)
            grads[n + 1, :, low] = jnp.where(mine, gaps[:WIDTH], gaps[WIDTH:]).astype(BF16)

    keep_y.wait()
    arrived(1, recv_y)
    lon_forward(recv_y, 1, dual)
    for part in range(2):
        rows = slice(HALF * part, HALF * part + HALF)
        back = matmul(dual[...], turned2[:, rows])
        pre[:, rows] = (back * slope[:, rows]).astype(BF16)
    outer(spec_t, pre, 0)
    outer(act_t, dual, 2)

    def share(k):
        return grads.at[k // 2, pl.ds(pl.multiple_of(lax.rem(k, 2) * 48, 16), 48), :]

    def to_owner(i):
        k = lax.rem(e + i, 8)
        return pltpu.make_async_remote_copy(
            src_ref=share(k),
            dst_ref=part1.at[e],
            send_sem=sum_out.at[i],
            recv_sem=sum_in.at[e],
            device_id=(dp, device_of(k, u)),
            device_id_type=MESH,
        )

    def send_shares():
        @pl.loop(1, 8)
        def _(i):
            to_owner(i).start()

    send_shares()

    for part in range(2):
        rows = slice(HALF * part, HALF * part + HALF)
        store_mixed(matmul(pre[...], turned1[:, rows]).astype(BF16), part)
    lon_inverse(2, back_y)

    def sum_shares():
        part1[e] = share(e)[...]

        @pl.loop(1, 8)
        def _(i):
            k = lax.rem(e + i, 8)
            pltpu.make_async_remote_copy(
                src_ref=part1.at[k],
                dst_ref=part1.at[k],
                send_sem=sum_out.at[i],
                recv_sem=sum_in.at[k],
                device_id=(dp, device_of(k, u)),
                device_id_type=MESH,
            ).wait_recv()

        total = part1[0].astype(F32)
        for k in range(1, 8):
            total = total + part1[k].astype(F32)
        total = total.astype(BF16)
        for t in range(TILES):
            a, b = t // 3, t % 3
            own1[t] = total[16 * a : 16 * a + 16, 128 * b : 128 * b + 128]

    sum_shares()
    heard(2)

    def place_of(t):
        return (16 * t) // TILES

    def reducer(t, h):
        return lax.rem(place_of(t) + 8 * h, 16) * 2 + lax.rem(t, 2)

    def near_reducer(t):
        far = lax.rem(z - place_of(t) + 20, 16) // 8
        return reducer(t, far)

    def to_reducer(t, h):
        return pltpu.make_async_remote_copy(
            src_ref=own1.at[t],
            dst_ref=part2.at[dp],
            send_sem=dp_out.at[2 * t + h],
            recv_sem=dp_in.at[dp],
            device_id=(reducer(t, h), me),
            device_id_type=MESH,
        )

    def each_reducer(act_on):
        @pl.loop(0, 2 * TILES)
        def _(n):
            t, h = n // 2, lax.rem(n, 2)

            @pl.when(dp != reducer(t, h))
            def _():
                act_on(to_reducer(t, h))

    def send_tiles():
        each_reducer(lambda copy: copy.start())

    send_tiles()
    start_all(to_cells, 2, back_x, home_x)
    keep_x = keep_back(back_x, home_x, 2)
    keep_x.start()
    start_all(to_cells, 3, back_y, home_y)
    keep_y = keep_back(back_y, home_y, 3)
    keep_y.start()

    def finish_cells(rows, home, out, n):
        for c in range(3):
            lanes = slice(256 * c, 256 * c + 256)
            got = matmul(lati[...], home[:, :, lanes].reshape(LAT * ROWS, 256))
            got = (got * SCALE).astype(BF16).astype(F32) + rows[:, lanes].astype(F32)
            rows[:, lanes] = got.astype(BF16)
        return pltpu.make_async_copy(rows, out, store_sem.at[n])


    spot = lax.rem(z, 8)
    mine = jnp.where(
        lax.rem(spot, 2) == 1,
        (spot + 1) // 2,
        jnp.where(spot == 0, 5 * side, 5 + spot // 2),
    )
    reduces = lax.rem(mine, 2) == side

    def neighbour(i):
        return lax.rem(z + i // 2 + 12, 16) * 2 + lax.rem(i, 2)

    def to_all(i):
        d = neighbour(i)
        return pltpu.make_async_remote_copy(
            src_ref=own3.at[mine],
            dst_ref=own3.at[mine],
            send_sem=cast_out.at[i],
            recv_sem=cast_in.at[mine],
            device_id=(d, me),
            device_id_type=MESH,
        )

    @pl.when(reduces)
    def _():
        part2[dp] = own1[mine]

        @pl.loop(1, dp_count)
        def _(i):
            d = lax.rem(dp + i, dp_count)
            pltpu.make_async_remote_copy(
                src_ref=part2.at[d],
                dst_ref=part2.at[d],
                send_sem=dp_out.at[0],
                recv_sem=dp_in.at[d],
                device_id=(d, me),
                device_id_type=MESH,
            ).wait_recv()

        whole = part2[0].astype(F32)
        for d in range(1, dp_count):
            whole = whole + part2[d].astype(F32)
        own3[mine] = (whole * (1.0 / SAMPLES)).astype(BF16)

        @pl.loop(0, 16)
        def _(i):
            @pl.when(neighbour(i) != dp)
            def _():
                to_all(i).start()

    keep_x.wait()
    arrived(2, home_x)
    store_x = finish_cells(xv, home_x, outx_hbm, 0)
    store_x.start()

    keep_y.wait()
    arrived(3, home_y)
    store_y = finish_cells(yv, home_y, outy_hbm, 1)
    store_y.start()

    @pl.loop(0, TILES)
    def _(t):
        @pl.when(dp != near_reducer(t))
        def _():
            pltpu.make_async_remote_copy(
                src_ref=own3.at[t],
                dst_ref=own3.at[t],
                send_sem=cast_out.at[0],
                recv_sem=cast_in.at[t],
                device_id=(near_reducer(t), me),
                device_id_type=MESH,
            ).wait_recv()

    twin = me + 1 - 2 * lax.rem(me, 2)

    def to_chips(i):
        return pltpu.make_async_remote_copy(
            src_ref=own3,
            dst_ref=final.at[me],
            send_sem=gather_out.at[i],
            recv_sem=gather_in.at[me],
            device_id=(dp, lax.rem(me + 2 * i, LON)),
            device_id_type=MESH,
        )

    def to_twin(i):
        s = lax.rem(me + 2 * i, LON)
        return pltpu.make_async_remote_copy(
            src_ref=final.at[s],
            dst_ref=final.at[s],
            send_sem=gather_out.at[8 + i],
            recv_sem=gather_in.at[s],
            device_id=(dp, twin),
            device_id_type=MESH,
        )

    def from_peer(s, sender):
        return pltpu.make_async_remote_copy(
            src_ref=final.at[s],
            dst_ref=final.at[s],
            send_sem=gather_out.at[0],
            recv_sem=gather_in.at[s],
            device_id=(dp, sender),
            device_id_type=MESH,
        )

    def gather_start():
        @pl.loop(1, 8)
        def _(i):
            to_chips(8 - i).start()

        final[me] = own3[...]
        to_twin(0).start()

    def gather_forward():
        @pl.loop(1, 8)
        def _(i):
            s = lax.rem(me + 2 * i, LON)
            from_peer(s, s).wait_recv()
            to_twin(i).start()

    def gather_wait():
        @pl.loop(0, 8)
        def _(i):
            from_peer(lax.rem(twin + 2 * i, LON), twin).wait_recv()

    def gather_sent():
        @pl.loop(1, 8)
        def _(i):
            to_chips(i).wait_send()
            to_twin(i).wait_send()

        to_twin(0).wait_send()

    gather_start()

    gather_forward()

    gather_wait()

    store_final = pltpu.make_async_copy(final, grads_hbm, store_sem.at[2])
    store_final.start()

    @pl.loop(1, LON)
    def _(i):
        to_mixer(0, send_x, recv_x, i).wait_send()
        to_mixer(1, send_y, recv_y, i).wait_send()
        to_cells(2, back_x, home_x, i).wait_send()
        to_cells(3, back_y, home_y, i).wait_send()

    def shares_sent():
        @pl.loop(1, 8)
        def _(i):
            to_owner(i).wait_send()

    shares_sent()
    gather_sent()

    each_reducer(lambda copy: copy.wait_send())

    @pl.when(reduces)
    def _():
        @pl.loop(0, 16)
        def _(i):
            @pl.when(neighbour(i) != dp)
            def _():
                to_all(i).wait_send()

    for store in [store_x, store_y, store_final]:
        store.wait()


def deliver(
    x_hbm, y_hbm, grads_hbm, outx_hbm, outy_hbm, grad1_hbm, grad2_hbm,
    xv, yv, final, strip, grad1, grad2, in_sem, out_sem,
):
    loads = [
        pltpu.make_async_copy(grads_hbm, final, in_sem.at[0]),
        pltpu.make_async_copy(x_hbm, xv, in_sem.at[1]),
        pltpu.make_async_copy(y_hbm, yv, in_sem.at[2]),
    ]
    for load in loads:
        load.start()
    stores = [
        pltpu.make_async_copy(xv, outx_hbm, out_sem.at[0]),
        pltpu.make_async_copy(yv, outy_hbm, out_sem.at[1]),
        pltpu.make_async_copy(grad1, grad1_hbm, out_sem.at[2]),
        pltpu.make_async_copy(grad2, grad2_hbm, out_sem.at[3]),
    ]
    loads[0].wait()
    for q in range(4):
        out = (grad1, grad2)[q // 2]
        for v in range(2):
            for t in range(2 * TILES):
                a, b = t // 3, t % 3
                tile = final[4 * q + 2 * v + a // 3, 3 * (a % 3) + b]
                strip[16 * a : 16 * a + 16, 128 * b : 128 * b + 128] = tile.astype(F32)
            for g in range(4):
                out[q % 2, 4 * v + g] = strip[:, WIDTH * g : WIDTH * g + WIDTH]
        if q < 2:
            loads[1 + q].wait()
            stores[q].start()
        if q % 2 == 1:
            stores[2 + q // 2].start()
    for store in stores:
        store.wait()


def on_device(fields, cotangent, first_weight, second_weight):
    dp_count = lax.axis_size("dp")
    rows = ROWS * LAT
    lon = jnp.asarray(lon_matrices(), BF16)
    lat = lat_matrix()
    lat_fwd, lat_inv = jnp.asarray(lat, BF16), jnp.asarray(lat.T.copy(), BF16)
    weight_shape = (2, GROUPS, WIDTH, WIDTH)
    any_spec = pl.BlockSpec(memory_space=pl.ANY)
    dma = pltpu.SemaphoreType.DMA
    cells = pltpu.VMEM((rows, CHANNELS), BF16)
    pairs = pltpu.VMEM((PAIRS, TILE, CHANNELS), BF16)
    lines = pltpu.VMEM((LINES, CHANNELS), BF16)
    blocks = pltpu.VMEM((OWN, LON, TILE, HALF), BF16)
    wide = pltpu.VMEM((CHANNELS, CHANNELS), BF16)
    turned = pltpu.VMEM((CHANNELS, LINES), BF16)
    side = 4 * MODES
    cell_shape = jax.ShapeDtypeStruct((rows, CHANNELS), BF16)
    grad_shape = jax.ShapeDtypeStruct(weight_shape, F32)
    final_shape = (LON, TILES, 16, 128)
    results = pl.pallas_call(
        kernel,
        out_shape=(cell_shape, cell_shape, jax.ShapeDtypeStruct(final_shape, BF16)),
        in_specs=[any_spec] * 7,
        out_specs=(any_spec,) * 3,
        scratch_shapes=[
            cells, cells,
            pltpu.VMEM(weight_shape, BF16), pltpu.VMEM(weight_shape, BF16),
            pltpu.VMEM((8, side, side), BF16),
            pltpu.VMEM((rows, rows), BF16), pltpu.VMEM((rows, rows), BF16),
            pairs, pairs, blocks, blocks, blocks, blocks, pairs, pairs,
            wide, wide, wide, wide,
            pltpu.VMEM((2, HALF, HALF), F32),
            lines, lines, lines, lines,
            pltpu.VMEM((LINES, CHANNELS), F32),
            pltpu.VMEM((OWN, side, HALF), BF16),
            turned, turned,
            pltpu.VMEM((4, WIDTH, HALF), BF16),
            pltpu.VMEM((8, 48, HALF), BF16),
            pltpu.VMEM((TILES, 16, 128), BF16),
            pltpu.VMEM((dp_count, 16, 128), BF16),
            pltpu.VMEM((TILES, 16, 128), BF16),
            pltpu.VMEM((LON, TILES, 16, 128), BF16),
            dma((8,)), dma((3,)), dma((4,)), dma((4, LON)), dma((4, LON)),
            dma((8,)), dma((8,)), dma((2 * TILES,)), dma((dp_count,)),
            dma((16,)), dma((TILES,)), dma((LON,)), dma((LON,)),
            pltpu.SemaphoreType.REGULAR((3,)),
        ],
        compiler_params=pltpu.CompilerParams(
            collective_id=0, has_side_effects=True, vmem_limit_bytes=63 << 20
        ),
    )(
        fields.reshape(rows, CHANNELS), cotangent.reshape(rows, CHANNELS),
        first_weight, second_weight, lon, lat_fwd, lat_inv,
    )
    wave, pull, grad1, grad2 = pl.pallas_call(
        deliver,
        out_shape=(cell_shape, cell_shape, grad_shape, grad_shape),
        in_specs=[any_spec] * 3,
        out_specs=(any_spec,) * 4,
        scratch_shapes=[
            cells, cells, pltpu.VMEM(final_shape, BF16), pltpu.VMEM((WIDTH, HALF), F32),
            pltpu.VMEM(weight_shape, F32), pltpu.VMEM(weight_shape, F32),
            dma((3,)), dma((4,)),
        ],
        compiler_params=pltpu.CompilerParams(vmem_limit_bytes=63 << 20),
    )(*results)
    shape = (1, ROWS, LAT, CHANNELS)
    return wave.reshape(shape), pull.reshape(shape), grad1, grad2


def solution(mesh):
    placed = (P("dp", "lon", None, None), P("dp", "lon", None, None), P(), P())
    return jax.shard_map(
        on_device, mesh=mesh, in_specs=placed, out_specs=placed, check_vma=False
    )
```

```python
import math

import jax
import jax.numpy as jnp
import ml_dtypes
import numpy as np
from jax import lax
from jax.experimental import pallas as pl
from jax.experimental.pallas import tpu as pltpu
from jax.sharding import PartitionSpec as P

COEF = 0.7978845608028654
CUBIC = 0.044715

SAMPLES = 32
CELLS = 128
LAT = 48
MODES = 64
CHANNELS = 768
GROUPS = 8
WIDTH = 96

LON = 16
ROWS = CELLS // LON
HALF = CHANNELS // 2
PAIRS = LAT // 2
OWN = PAIRS // (LON // 2)
TILE = 2 * ROWS
LINES = OWN * 2 * MODES
TILES = 9
SCALE = 1.0 / math.sqrt(CELLS * LAT)
MESH = pl.DeviceIdType.MESH
BF16 = jnp.bfloat16
F32 = jnp.float32


def make_basis(length, count):
    product = np.arange(length)[:, None] * np.arange(count)[None, :] % length
    angle = product.astype(np.float32) * np.float32(2.0 * math.pi / length)
    table = np.stack([np.cos(angle), -np.sin(angle)], axis=-1)
    return table.astype(ml_dtypes.bfloat16).astype(np.float32)


def lat_matrix():
    table = make_basis(LAT, LAT)
    half = np.zeros((PAIRS, 2, LAT), np.float32)
    half[0, 0] = table[:, 0, 0]
    half[0, 1] = table[:, PAIRS, 0]
    for j in range(1, PAIRS):
        half[j, 0] = table[:, j, 0]
        half[j, 1] = table[:, j, 1]
    full = np.einsum("pah,wv->pawvh", half, np.eye(ROWS, dtype=np.float32))
    return full.reshape(PAIRS * 2 * ROWS, ROWS * LAT)


def lon_matrix(special, weighted):
    table = make_basis(CELLS, MODES)
    cos, sin = table[:, :, 0].T, table[:, :, 1].T
    if weighted:
        factor = np.where(np.arange(MODES) == 0, 1.0, 2.0).astype(np.float32)[:, None]
        cos, sin = cos * factor, sin * factor
    zero = np.zeros_like(cos)
    if special:
        from_real = [cos, sin, zero, zero]
        from_imag = [zero, zero, cos, sin]
    else:
        from_real = [cos, sin, cos, sin]
        from_imag = [-sin, cos, sin, -cos]
    both = np.stack([np.concatenate(from_real), np.concatenate(from_imag)], axis=1)
    both = both.reshape(4 * MODES, 2, LON, ROWS).transpose(0, 2, 1, 3)
    return both.reshape(4 * MODES, 2 * CELLS)


def lon_matrices():
    found = []
    for special in (False, True):
        plain, weighted = lon_matrix(special, False), lon_matrix(special, True)
        found += [plain, weighted, plain.T, weighted.T]
    return np.stack(found)


def matmul(left, right):
    return jnp.dot(left, right, preferred_element_type=F32)


def kernel(
    x_hbm, y_hbm, w1_hbm, w2_hbm, lon_hbm, latf_hbm, lati_hbm,
    outx_hbm, outy_hbm, grads_hbm,
    xv, yv, w1v, w2v, lonv, latf, lati,
    send_x, send_y, recv_x, recv_y, back_x, back_y, home_x, home_y,
    wide1, wide2, turned1, turned2, place, spec, dual, act, pre, slope, mixed,
    spec_t, act_t, grads, part1, own1, part2, own3, final,
    load_sem, store_sem, self_sem, out_sem, in_sem,
    sum_out, sum_in, dp_out, dp_in, cast_out, cast_in, gather_out, gather_in, relay,
):
    dp_count = lax.axis_size("dp")
    me, dp = lax.axis_index("lon"), lax.axis_index("dp")
    ring, z, side = dp_count // 2, dp // 2, lax.rem(dp, 2)

    def half_of(s):
        return lax.rem(s // 2, 2)

    def slot_of(s):
        return (s // 4) * 2 + lax.rem(s, 2)

    def device_of(e, u):
        return (e // 2) * 4 + u * 2 + lax.rem(e, 2)

    u, e = half_of(me), slot_of(me)
    first = jnp.where(e == 0, 4, 0)

    loads = [
        pltpu.make_async_copy(x_hbm, xv, load_sem.at[0]),
        pltpu.make_async_copy(latf_hbm, latf, load_sem.at[1]),
        pltpu.make_async_copy(y_hbm, yv, load_sem.at[2]),
        pltpu.make_async_copy(w1_hbm, w1v, load_sem.at[3]),
        pltpu.make_async_copy(w2_hbm, w2v, load_sem.at[4]),
        pltpu.make_async_copy(lon_hbm.at[pl.ds(0, 4)], lonv.at[pl.ds(0, 4)], load_sem.at[5]),
        pltpu.make_async_copy(lon_hbm.at[pl.ds(first, 4)], lonv.at[pl.ds(4, 4)], load_sem.at[6]),
        pltpu.make_async_copy(lati_hbm, lati, load_sem.at[7]),
    ]
    barrier = pltpu.get_barrier_semaphore()

    @pl.loop(1, LON)
    def _(i):
        pl.semaphore_signal(
            barrier, inc=1, device_id=(dp, lax.rem(me + i, LON)), device_id_type=MESH
        )

    def along(step):
        return lax.rem(z + step + ring, ring) * 2 + side

    turn = 1 - 2 * side
    for other in (along(1), along(-1), dp + turn, along(1) + turn, along(-1) + turn):
        pl.semaphore_signal(barrier, inc=1, device_id=(other, me), device_id_type=MESH)

    for load in loads:
        load.start()

    def announce(r):
        for step in (2**r, -(2**r)):
            pl.semaphore_signal(
                relay.at[r], inc=1, device_id=(along(step), me), device_id_type=MESH
            )

    def heard(r):
        pl.semaphore_wait(relay.at[r], 2)

    def lat_forward(rows, out):
        for n in range(3):
            lanes = slice(256 * n, 256 * n + 256)
            got = matmul(latf[...], rows[:, lanes]).astype(BF16)
            out[:, :, lanes] = got.reshape(PAIRS, TILE, 256)

    def block_of(buf, s):
        lanes = pl.ds(pl.multiple_of(half_of(s) * HALF, 128), HALF)
        return buf.at[pl.ds(slot_of(s) * OWN, OWN), :, lanes]

    def to_mixer(stage, src, dst, i):
        s = lax.rem(me + i, LON)
        return pltpu.make_async_remote_copy(
            src_ref=block_of(src, s),
            dst_ref=dst.at[:, me],
            send_sem=out_sem.at[stage, i],
            recv_sem=in_sem.at[stage, me],
            device_id=(dp, s),
            device_id_type=MESH,
        )

    def to_cells(stage, src, dst, i):
        s = lax.rem(me + i, LON)
        return pltpu.make_async_remote_copy(
            src_ref=src.at[:, s],
            dst_ref=block_of(dst, me),
            send_sem=out_sem.at[stage, i],
            recv_sem=in_sem.at[stage, me],
            device_id=(dp, s),
            device_id_type=MESH,
        )

    def start_all(make, stage, src, dst):
        @pl.loop(1, LON)
        def _(i):
            make(stage, src, dst, LON - i).start()

    def arrived(stage, buf):
        @pl.loop(1, LON)
        def _(i):
            s = lax.rem(me + i, LON)
            if stage < 2:
                spot = buf.at[:, s]
            else:
                spot = block_of(buf, s)
            pltpu.make_async_remote_copy(
                src_ref=spot,
                dst_ref=spot,
                send_sem=out_sem.at[stage, i],
                recv_sem=in_sem.at[stage, s],
                device_id=(dp, s),
                device_id_type=MESH,
            ).wait_recv()

    def keep_forward(src, dst, n):
        return pltpu.make_async_copy(block_of(src, me), dst.at[:, me], self_sem.at[n])

    def keep_back(src, dst, n):
        return pltpu.make_async_copy(src.at[:, me], block_of(dst, me), self_sem.at[n])

    loads[0].wait()
    loads[1].wait()
    lat_forward(xv, send_x)
    pl.semaphore_wait(barrier, LON - 1 + 5)
    start_all(to_mixer, 0, send_x, recv_x)
    keep_x = keep_forward(send_x, recv_x, 0)
    keep_x.start()
    loads[2].wait()
    lat_forward(yv, send_y)
    start_all(to_mixer, 1, send_y, recv_y)
    keep_y = keep_forward(send_y, recv_y, 1)
    keep_y.start()
    announce(0)

    def widen(weight, wide, turned):
        for p in range(2):
            for g in range(4):
                own = slice(WIDTH * g, WIDTH * g + WIDTH)
                place[p, own, own] = weight[p, 4 * u + g].astype(F32)
        real, imag = place[0].astype(BF16), place[1].astype(BF16)
        wide[:HALF, :HALF] = real
        wide[HALF:, HALF:] = real
        wide[:HALF, HALF:] = imag
        wide[HALF:, :HALF] = -imag
        real, imag = place[0].T.astype(BF16), place[1].T.astype(BF16)
        turned[:HALF, :HALF] = real
        turned[HALF:, HALF:] = real
        turned[:HALF, HALF:] = -imag
        turned[HALF:, :HALF] = imag

    place[...] = jnp.zeros_like(place)
    for load in loads[3:]:
        load.wait()
    widen(w1v, wide1, turned1)
    widen(w2v, wide2, turned2)
    heard(0)
    announce(1)

    def lon_forward(buf, kind, out):
        for p in range(OWN):
            table = lonv[kind + (4 if p == 0 else 0)]
            got = matmul(table, buf[p].reshape(2 * CELLS, HALF))
            got = (got * SCALE).astype(BF16)
            for x in range(2):
                rows = slice((2 * p + x) * MODES, (2 * p + x + 1) * MODES)
                out[rows, :HALF] = got[2 * x * MODES : (2 * x + 1) * MODES]
                out[rows, HALF:] = got[(2 * x + 1) * MODES : (2 * x + 2) * MODES]

    def store_mixed(got, part):
        for p in range(OWN):
            for x in range(2):
                rows = slice((2 * p + x) * MODES, (2 * p + x + 1) * MODES)
                to = slice((2 * x + part) * MODES, (2 * x + part + 1) * MODES)
                mixed[p, to, :] = got[rows]

    def lon_inverse(kind, out):
        for p in range(OWN):
            table = lonv[kind + (4 if p == 0 else 0)]
            got = matmul(table, mixed[p]).astype(BF16)
            out[p] = got.reshape(LON, TILE, HALF)

    keep_x.wait()
    arrived(0, recv_x)
    lon_forward(recv_x, 0, spec)
    for part in range(2):
        lanes = slice(HALF * part, HALF * part + HALF)
        inner = matmul(spec[...], wide1[:, lanes])
        hyper = jnp.tanh(COEF * (inner + CUBIC * inner * inner * inner))
        act[:, lanes] = (0.5 * inner * (1.0 + hyper)).astype(BF16)
        slope[:, lanes] = 0.5 * (1.0 + hyper) + 0.5 * inner * (1.0 - hyper * hyper) * COEF * (
            1.0 + 3.0 * CUBIC * inner * inner
        )
    for part in range(2):
        lanes = slice(HALF * part, HALF * part + HALF)
        store_mixed(matmul(act[...], wide2[:, lanes]).astype(BF16), part)
    lon_inverse(3, back_x)

    heard(1)
    announce(2)

    spec_t[...] = spec[...].T
    act_t[...] = act[...].T

    def outer(left_t, right, n):
        lane = lax.broadcasted_iota(jnp.int32, (WIDTH, 128), 1)
        for b in range(3):
            low = slice(128 * b, 128 * b + 128)
            high = slice(HALF + 128 * b, HALF + 128 * b + 128)
            columns = jnp.concatenate([right[:, low], right[:, high]], axis=1)
            span = 2 * WIDTH
            top = matmul(left_t[WIDTH * b : WIDTH * b + span, :], columns)
            bottom = matmul(left_t[HALF + WIDTH * b : HALF + WIDTH * b + span, :], columns)
            sums = top[:, :128] + bottom[:, 128:]
            gaps = top[:, 128:] - bottom[:, :128]
            mine = lane < WIDTH - 32 * b
            grads[n, :, low] = jnp.where(mine, sums[:WIDTH], sums[WIDTH:]).astype(BF16)
            grads[n + 1, :, low] = jnp.where(mine, gaps[:WIDTH], gaps[WIDTH:]).astype(BF16)

    def share(k):
        return grads.at[k // 2, pl.ds(pl.multiple_of(lax.rem(k, 2) * 48, 16), 48), :]

    def to_owner(k):
        return pltpu.make_async_remote_copy(
            src_ref=share(k),
            dst_ref=part1.at[e],
            send_sem=sum_out.at[k],
            recv_sem=sum_in.at[e],
            device_id=(dp, device_of(k, u)),
            device_id_type=MESH,
        )

    def each_owner(low, act_on):
        @pl.loop(0, 4)
        def _(i):
            k = low + lax.rem(e + 2 + i, 4)

            @pl.when(k != e)
            def _():
                act_on(to_owner(k))

    def start(copy):
        copy.start()

    keep_y.wait()
    arrived(1, recv_y)
    lon_forward(recv_y, 1, dual)
    outer(act_t, dual, 2)
    each_owner(4, start)
    for part in range(2):
        rows = slice(HALF * part, HALF * part + HALF)
        back = matmul(dual[...], turned2[:, rows])
        pre[:, rows] = (back * slope[:, rows]).astype(BF16)
    outer(spec_t, pre, 0)
    each_owner(0, start)

    for part in range(2):
        rows = slice(HALF * part, HALF * part + HALF)
        store_mixed(matmul(pre[...], turned1[:, rows]).astype(BF16), part)
    lon_inverse(2, back_y)

    def sum_shares():
        part1[e] = share(e)[...]

        @pl.loop(1, 8)
        def _(i):
            k = lax.rem(e + i, 8)
            pltpu.make_async_remote_copy(
                src_ref=part1.at[k],
                dst_ref=part1.at[k],
                send_sem=sum_out.at[k],
                recv_sem=sum_in.at[k],
                device_id=(dp, device_of(k, u)),
                device_id_type=MESH,
            ).wait_recv()

        total = part1[0].astype(F32)
        for k in range(1, 8):
            total = total + part1[k].astype(F32)
        total = total.astype(BF16)
        for t in range(TILES):
            a, b = t // 3, t % 3
            own1[t] = total[16 * a : 16 * a + 16, 128 * b : 128 * b + 128]

    sum_shares()
    heard(2)

    def place_of(t):
        return (16 * t) // TILES

    def reducer(t, h):
        return lax.rem(place_of(t) + 8 * h, 16) * 2 + lax.rem(t, 2)

    def near_reducer(t):
        far = lax.rem(z - place_of(t) + 20, 16) // 8
        return reducer(t, far)

    def to_reducer(t, h):
        return pltpu.make_async_remote_copy(
            src_ref=own1.at[t],
            dst_ref=part2.at[dp],
            send_sem=dp_out.at[2 * t + h],
            recv_sem=dp_in.at[dp],
            device_id=(reducer(t, h), me),
            device_id_type=MESH,
        )

    def each_reducer(act_on):
        @pl.loop(0, 2 * TILES)
        def _(n):
            t, h = n // 2, lax.rem(n, 2)

            @pl.when(dp != reducer(t, h))
            def _():
                act_on(to_reducer(t, h))

    def send_tiles():
        each_reducer(lambda copy: copy.start())

    send_tiles()
    start_all(to_cells, 2, back_x, home_x)
    keep_x = keep_back(back_x, home_x, 2)
    keep_x.start()
    start_all(to_cells, 3, back_y, home_y)
    keep_y = keep_back(back_y, home_y, 3)
    keep_y.start()

    @pl.loop(1, LON)
    def _(i):
        to_mixer(0, send_x, recv_x, i).wait_send()
        to_mixer(1, send_y, recv_y, i).wait_send()

    for low in (0, 4):
        each_owner(low, lambda copy: copy.wait_send())

    def finish_cells(rows, home, out, n):
        for c in range(3):
            lanes = slice(256 * c, 256 * c + 256)
            got = matmul(lati[...], home[:, :, lanes].reshape(LAT * ROWS, 256))
            got = (got * SCALE).astype(BF16).astype(F32) + rows[:, lanes].astype(F32)
            rows[:, lanes] = got.astype(BF16)
        return pltpu.make_async_copy(rows, out, store_sem.at[n])


    spot = lax.rem(z, 8)
    mine = jnp.where(
        lax.rem(spot, 2) == 1,
        (spot + 1) // 2,
        jnp.where(spot == 0, 5 * side, 5 + spot // 2),
    )
    reduces = lax.rem(mine, 2) == side

    def neighbour(i):
        return lax.rem(z + i // 2 + 12, 16) * 2 + lax.rem(i, 2)

    def to_all(i):
        d = neighbour(i)
        return pltpu.make_async_remote_copy(
            src_ref=own3.at[mine],
            dst_ref=own3.at[mine],
            send_sem=cast_out.at[i],
            recv_sem=cast_in.at[mine],
            device_id=(d, me),
            device_id_type=MESH,
        )

    @pl.when(reduces)
    def _():
        part2[dp] = own1[mine]

        @pl.loop(1, dp_count)
        def _(i):
            d = lax.rem(dp + i, dp_count)
            pltpu.make_async_remote_copy(
                src_ref=part2.at[d],
                dst_ref=part2.at[d],
                send_sem=dp_out.at[0],
                recv_sem=dp_in.at[d],
                device_id=(d, me),
                device_id_type=MESH,
            ).wait_recv()

        whole = part2[0].astype(F32)
        for d in range(1, dp_count):
            whole = whole + part2[d].astype(F32)
        own3[mine] = (whole * (1.0 / SAMPLES)).astype(BF16)

        @pl.loop(0, 16)
        def _(i):
            @pl.when(neighbour(i) != dp)
            def _():
                to_all(i).start()

    keep_x.wait()
    arrived(2, home_x)
    store_x = finish_cells(xv, home_x, outx_hbm, 0)
    store_x.start()

    keep_y.wait()
    arrived(3, home_y)
    store_y = finish_cells(yv, home_y, outy_hbm, 1)
    store_y.start()

    @pl.loop(0, TILES)
    def _(t):
        @pl.when(dp != near_reducer(t))
        def _():
            pltpu.make_async_remote_copy(
                src_ref=own3.at[t],
                dst_ref=own3.at[t],
                send_sem=cast_out.at[0],
                recv_sem=cast_in.at[t],
                device_id=(near_reducer(t), me),
                device_id_type=MESH,
            ).wait_recv()

    twin = me + 1 - 2 * lax.rem(me, 2)

    def to_chips(i):
        return pltpu.make_async_remote_copy(
            src_ref=own3,
            dst_ref=final.at[me],
            send_sem=gather_out.at[i],
            recv_sem=gather_in.at[me],
            device_id=(dp, lax.rem(me + 2 * i, LON)),
            device_id_type=MESH,
        )

    def to_twin(i):
        s = lax.rem(me + 2 * i, LON)
        return pltpu.make_async_remote_copy(
            src_ref=final.at[s],
            dst_ref=final.at[s],
            send_sem=gather_out.at[8 + i],
            recv_sem=gather_in.at[s],
            device_id=(dp, twin),
            device_id_type=MESH,
        )

    def from_peer(s, sender):
        return pltpu.make_async_remote_copy(
            src_ref=final.at[s],
            dst_ref=final.at[s],
            send_sem=gather_out.at[0],
            recv_sem=gather_in.at[s],
            device_id=(dp, sender),
            device_id_type=MESH,
        )

    def gather_start():
        @pl.loop(1, 8)
        def _(i):
            to_chips(8 - i).start()

        final[me] = own3[...]
        to_twin(0).start()

    def gather_forward():
        @pl.loop(1, 8)
        def _(i):
            s = lax.rem(me + 2 * i, LON)
            from_peer(s, s).wait_recv()
            to_twin(i).start()

    def gather_wait():
        @pl.loop(0, 8)
        def _(i):
            from_peer(lax.rem(twin + 2 * i, LON), twin).wait_recv()

    def gather_sent():
        @pl.loop(1, 8)
        def _(i):
            to_chips(i).wait_send()
            to_twin(i).wait_send()

        to_twin(0).wait_send()

    gather_start()

    @pl.loop(1, LON)
    def _(i):
        to_cells(2, back_x, home_x, i).wait_send()
        to_cells(3, back_y, home_y, i).wait_send()

    each_reducer(lambda copy: copy.wait_send())

    @pl.when(reduces)
    def _():
        @pl.loop(0, 16)
        def _(i):
            @pl.when(neighbour(i) != dp)
            def _():
                to_all(i).wait_send()

    gather_forward()

    gather_wait()

    store_final = pltpu.make_async_copy(final, grads_hbm, store_sem.at[2])
    store_final.start()

    gather_sent()
    for store in [store_x, store_y, store_final]:
        store.wait()


def deliver(
    x_hbm, y_hbm, grads_hbm, outx_hbm, outy_hbm, grad1_hbm, grad2_hbm,
    xv, yv, final, strip, grad1, grad2, in_sem, out_sem,
):
    loads = [
        pltpu.make_async_copy(grads_hbm, final, in_sem.at[0]),
        pltpu.make_async_copy(x_hbm, xv, in_sem.at[1]),
        pltpu.make_async_copy(y_hbm, yv, in_sem.at[2]),
    ]
    for load in loads:
        load.start()
    stores = [
        pltpu.make_async_copy(xv, outx_hbm, out_sem.at[0]),
        pltpu.make_async_copy(yv, outy_hbm, out_sem.at[1]),
        pltpu.make_async_copy(grad1, grad1_hbm, out_sem.at[2]),
        pltpu.make_async_copy(grad2, grad2_hbm, out_sem.at[3]),
    ]
    loads[0].wait()
    for q in range(4):
        out = (grad1, grad2)[q // 2]
        for v in range(2):
            for t in range(2 * TILES):
                a, b = t // 3, t % 3
                tile = final[4 * q + 2 * v + a // 3, 3 * (a % 3) + b]
                strip[16 * a : 16 * a + 16, 128 * b : 128 * b + 128] = tile.astype(F32)
            for g in range(4):
                out[q % 2, 4 * v + g] = strip[:, WIDTH * g : WIDTH * g + WIDTH]
        if q < 2:
            loads[1 + q].wait()
            stores[q].start()
        if q % 2 == 1:
            stores[2 + q // 2].start()
    for store in stores:
        store.wait()


def on_device(fields, cotangent, first_weight, second_weight):
    dp_count = lax.axis_size("dp")
    rows = ROWS * LAT
    lon = jnp.asarray(lon_matrices(), BF16)
    lat = lat_matrix()
    lat_fwd, lat_inv = jnp.asarray(lat, BF16), jnp.asarray(lat.T.copy(), BF16)
    weight_shape = (2, GROUPS, WIDTH, WIDTH)
    any_spec = pl.BlockSpec(memory_space=pl.ANY)
    dma = pltpu.SemaphoreType.DMA
    cells = pltpu.VMEM((rows, CHANNELS), BF16)
    pairs = pltpu.VMEM((PAIRS, TILE, CHANNELS), BF16)
    lines = pltpu.VMEM((LINES, CHANNELS), BF16)
    blocks = pltpu.VMEM((OWN, LON, TILE, HALF), BF16)
    wide = pltpu.VMEM((CHANNELS, CHANNELS), BF16)
    turned = pltpu.VMEM((CHANNELS, LINES), BF16)
    side = 4 * MODES
    cell_shape = jax.ShapeDtypeStruct((rows, CHANNELS), BF16)
    grad_shape = jax.ShapeDtypeStruct(weight_shape, F32)
    final_shape = (LON, TILES, 16, 128)
    results = pl.pallas_call(
        kernel,
        out_shape=(cell_shape, cell_shape, jax.ShapeDtypeStruct(final_shape, BF16)),
        in_specs=[any_spec] * 7,
        out_specs=(any_spec,) * 3,
        scratch_shapes=[
            cells, cells,
            pltpu.VMEM(weight_shape, BF16), pltpu.VMEM(weight_shape, BF16),
            pltpu.VMEM((8, side, side), BF16),
            pltpu.VMEM((rows, rows), BF16), pltpu.VMEM((rows, rows), BF16),
            pairs, pairs, blocks, blocks, blocks, blocks, pairs, pairs,
            wide, wide, wide, wide,
            pltpu.VMEM((2, HALF, HALF), F32),
            lines, lines, lines, lines,
            pltpu.VMEM((LINES, CHANNELS), F32),
            pltpu.VMEM((OWN, side, HALF), BF16),
            turned, turned,
            pltpu.VMEM((4, WIDTH, HALF), BF16),
            pltpu.VMEM((8, 48, HALF), BF16),
            pltpu.VMEM((TILES, 16, 128), BF16),
            pltpu.VMEM((dp_count, 16, 128), BF16),
            pltpu.VMEM((TILES, 16, 128), BF16),
            pltpu.VMEM((LON, TILES, 16, 128), BF16),
            dma((8,)), dma((3,)), dma((4,)), dma((4, LON)), dma((4, LON)),
            dma((8,)), dma((8,)), dma((2 * TILES,)), dma((dp_count,)),
            dma((16,)), dma((TILES,)), dma((LON,)), dma((LON,)),
            pltpu.SemaphoreType.REGULAR((3,)),
        ],
        compiler_params=pltpu.CompilerParams(
            collective_id=0, has_side_effects=True, vmem_limit_bytes=63 << 20
        ),
    )(
        fields.reshape(rows, CHANNELS), cotangent.reshape(rows, CHANNELS),
        first_weight, second_weight, lon, lat_fwd, lat_inv,
    )
    wave, pull, grad1, grad2 = pl.pallas_call(
        deliver,
        out_shape=(cell_shape, cell_shape, grad_shape, grad_shape),
        in_specs=[any_spec] * 3,
        out_specs=(any_spec,) * 4,
        scratch_shapes=[
            cells, cells, pltpu.VMEM(final_shape, BF16), pltpu.VMEM((WIDTH, HALF), F32),
            pltpu.VMEM(weight_shape, F32), pltpu.VMEM(weight_shape, F32),
            dma((3,)), dma((4,)),
        ],
        compiler_params=pltpu.CompilerParams(vmem_limit_bytes=63 << 20),
    )(*results)
    shape = (1, ROWS, LAT, CHANNELS)
    return wave.reshape(shape), pull.reshape(shape), grad1, grad2


def solution(mesh):
    placed = (P("dp", "lon", None, None), P("dp", "lon", None, None), P(), P())
    return jax.shard_map(
        on_device, mesh=mesh, in_specs=placed, out_specs=placed, check_vma=False
    )
```

```python
import math

import jax
import jax.numpy as jnp
import ml_dtypes
import numpy as np
from jax import lax
from jax.experimental import pallas as pl
from jax.experimental.pallas import tpu as pltpu
from jax.sharding import PartitionSpec as P

COEF = 0.7978845608028654
CUBIC = 0.044715

SAMPLES = 32
CELLS = 128
LAT = 48
MODES = 64
CHANNELS = 768
GROUPS = 8
WIDTH = 96

LON = 16
ROWS = CELLS // LON
HALF = CHANNELS // 2
PAIRS = LAT // 2
OWN = PAIRS // (LON // 2)
TILE = 2 * ROWS
LINES = OWN * 2 * MODES
TILES = 9
SCALE = 1.0 / math.sqrt(CELLS * LAT)
MESH = pl.DeviceIdType.MESH
BF16 = jnp.bfloat16
F32 = jnp.float32


def make_basis(length, count):
    product = np.arange(length)[:, None] * np.arange(count)[None, :] % length
    angle = product.astype(np.float32) * np.float32(2.0 * math.pi / length)
    table = np.stack([np.cos(angle), -np.sin(angle)], axis=-1)
    return table.astype(ml_dtypes.bfloat16).astype(np.float32)


def lat_matrix():
    table = make_basis(LAT, LAT)
    half = np.zeros((PAIRS, 2, LAT), np.float32)
    half[0, 0] = table[:, 0, 0]
    half[0, 1] = table[:, PAIRS, 0]
    for j in range(1, PAIRS):
        half[j, 0] = table[:, j, 0]
        half[j, 1] = table[:, j, 1]
    full = np.einsum("pah,wv->pawvh", half, np.eye(ROWS, dtype=np.float32))
    return full.reshape(PAIRS * 2 * ROWS, ROWS * LAT)


def lon_matrix(special, weighted):
    table = make_basis(CELLS, MODES)
    cos, sin = table[:, :, 0].T, table[:, :, 1].T
    if weighted:
        factor = np.where(np.arange(MODES) == 0, 1.0, 2.0).astype(np.float32)[:, None]
        cos, sin = cos * factor, sin * factor
    zero = np.zeros_like(cos)
    if special:
        from_real = [cos, sin, zero, zero]
        from_imag = [zero, zero, cos, sin]
    else:
        from_real = [cos, sin, cos, sin]
        from_imag = [-sin, cos, sin, -cos]
    both = np.stack([np.concatenate(from_real), np.concatenate(from_imag)], axis=1)
    both = both.reshape(4 * MODES, 2, LON, ROWS).transpose(0, 2, 1, 3)
    return both.reshape(4 * MODES, 2 * CELLS)


def lon_matrices():
    found = []
    for special in (False, True):
        plain, weighted = lon_matrix(special, False), lon_matrix(special, True)
        found += [plain, weighted, plain.T, weighted.T]
    return np.stack(found)


def matmul(left, right):
    return jnp.dot(left, right, preferred_element_type=F32)


def kernel(
    x_hbm, y_hbm, w1_hbm, w2_hbm, lon_hbm, latf_hbm, lati_hbm,
    outx_hbm, outy_hbm, grads_hbm,
    xv, yv, w1v, w2v, lonv, latf, lati,
    send_x, send_y, recv_x, recv_y, back_x, back_y, home_x, home_y,
    wide1, wide2, turned1, turned2, place, spec, dual, act, pre, slope, mixed,
    spec_t, act_t, grads, part1, own1, part2, own3, final,
    load_sem, store_sem, self_sem, out_sem, in_sem,
    sum_out, sum_in, dp_out, dp_in, cast_out, cast_in, gather_out, gather_in, relay,
):
    dp_count = lax.axis_size("dp")
    me, dp = lax.axis_index("lon"), lax.axis_index("dp")
    ring, z, side = dp_count // 2, dp // 2, lax.rem(dp, 2)

    def half_of(s):
        return lax.rem(s // 2, 2)

    def slot_of(s):
        return (s // 4) * 2 + lax.rem(s, 2)

    def device_of(e, u):
        return (e // 2) * 4 + u * 2 + lax.rem(e, 2)

    u, e = half_of(me), slot_of(me)
    first = jnp.where(e == 0, 4, 0)

    loads = [
        pltpu.make_async_copy(x_hbm, xv, load_sem.at[0]),
        pltpu.make_async_copy(latf_hbm, latf, load_sem.at[1]),
        pltpu.make_async_copy(y_hbm, yv, load_sem.at[2]),
        pltpu.make_async_copy(w1_hbm, w1v, load_sem.at[3]),
        pltpu.make_async_copy(w2_hbm, w2v, load_sem.at[4]),
        pltpu.make_async_copy(lon_hbm.at[pl.ds(0, 4)], lonv.at[pl.ds(0, 4)], load_sem.at[5]),
        pltpu.make_async_copy(lon_hbm.at[pl.ds(first, 4)], lonv.at[pl.ds(4, 4)], load_sem.at[6]),
        pltpu.make_async_copy(lati_hbm, lati, load_sem.at[7]),
    ]
    barrier = pltpu.get_barrier_semaphore()

    @pl.loop(1, LON)
    def _(i):
        pl.semaphore_signal(
            barrier, inc=1, device_id=(dp, lax.rem(me + i, LON)), device_id_type=MESH
        )

    def along(step):
        return lax.rem(z + step + ring, ring) * 2 + side

    turn = 1 - 2 * side
    for other in (along(1), along(-1), dp + turn, along(1) + turn, along(-1) + turn):
        pl.semaphore_signal(barrier, inc=1, device_id=(other, me), device_id_type=MESH)

    for load in loads:
        load.start()

    def announce(r):
        for step in (2**r, -(2**r)):
            pl.semaphore_signal(
                relay.at[r], inc=1, device_id=(along(step), me), device_id_type=MESH
            )

    def heard(r):
        pl.semaphore_wait(relay.at[r], 2)

    def lat_forward(rows, out):
        for n in range(3):
            lanes = slice(256 * n, 256 * n + 256)
            got = matmul(latf[...], rows[:, lanes]).astype(BF16)
            out[:, :, lanes] = got.reshape(PAIRS, TILE, 256)

    def block_of(buf, s):
        lanes = pl.ds(pl.multiple_of(half_of(s) * HALF, 128), HALF)
        return buf.at[pl.ds(slot_of(s) * OWN, OWN), :, lanes]

    def to_mixer(stage, src, dst, i):
        s = lax.rem(me + i, LON)
        return pltpu.make_async_remote_copy(
            src_ref=block_of(src, s),
            dst_ref=dst.at[:, me],
            send_sem=out_sem.at[stage, i],
            recv_sem=in_sem.at[stage, me],
            device_id=(dp, s),
            device_id_type=MESH,
        )

    def to_cells(stage, src, dst, i):
        s = lax.rem(me + i, LON)
        return pltpu.make_async_remote_copy(
            src_ref=src.at[:, s],
            dst_ref=block_of(dst, me),
            send_sem=out_sem.at[stage, i],
            recv_sem=in_sem.at[stage, me],
            device_id=(dp, s),
            device_id_type=MESH,
        )

    def start_all(make, stage, src, dst):
        @pl.loop(1, LON)
        def _(i):
            make(stage, src, dst, LON - i).start()

    def arrived(stage, buf):
        @pl.loop(1, LON)
        def _(i):
            s = lax.rem(me + i, LON)
            if stage < 2:
                spot = buf.at[:, s]
            else:
                spot = block_of(buf, s)
            pltpu.make_async_remote_copy(
                src_ref=spot,
                dst_ref=spot,
                send_sem=out_sem.at[stage, i],
                recv_sem=in_sem.at[stage, s],
                device_id=(dp, s),
                device_id_type=MESH,
            ).wait_recv()

    def keep_forward(src, dst, n):
        return pltpu.make_async_copy(block_of(src, me), dst.at[:, me], self_sem.at[n])

    def keep_back(src, dst, n):
        return pltpu.make_async_copy(src.at[:, me], block_of(dst, me), self_sem.at[n])

    loads[0].wait()
    loads[1].wait()
    lat_forward(xv, send_x)
    pl.semaphore_wait(barrier, LON - 1 + 5)
    start_all(to_mixer, 0, send_x, recv_x)
    keep_x = keep_forward(send_x, recv_x, 0)
    keep_x.start()
    loads[2].wait()
    lat_forward(yv, send_y)
    start_all(to_mixer, 1, send_y, recv_y)
    keep_y = keep_forward(send_y, recv_y, 1)
    keep_y.start()
    announce(0)

    def widen(weight, wide, turned):
        for p in range(2):
            for g in range(4):
                own = slice(WIDTH * g, WIDTH * g + WIDTH)
                place[p, own, own] = weight[p, 4 * u + g].astype(F32)
        real, imag = place[0].astype(BF16), place[1].astype(BF16)
        wide[:HALF, :HALF] = real
        wide[HALF:, HALF:] = real
        wide[:HALF, HALF:] = imag
        wide[HALF:, :HALF] = -imag
        real, imag = place[0].T.astype(BF16), place[1].T.astype(BF16)
        turned[:HALF, :HALF] = real
        turned[HALF:, HALF:] = real
        turned[:HALF, HALF:] = -imag
        turned[HALF:, :HALF] = imag

    place[...] = jnp.zeros_like(place)
    for load in loads[3:]:
        load.wait()
    widen(w1v, wide1, turned1)
    widen(w2v, wide2, turned2)
    heard(0)
    announce(1)

    def lon_forward(buf, kind, out):
        for p in range(OWN):
            table = lonv[kind + (4 if p == 0 else 0)]
            got = matmul(table, buf[p].reshape(2 * CELLS, HALF))
            got = (got * SCALE).astype(BF16)
            for x in range(2):
                rows = slice((2 * p + x) * MODES, (2 * p + x + 1) * MODES)
                out[rows, :HALF] = got[2 * x * MODES : (2 * x + 1) * MODES]
                out[rows, HALF:] = got[(2 * x + 1) * MODES : (2 * x + 2) * MODES]

    def store_mixed(got, part):
        for p in range(OWN):
            for x in range(2):
                rows = slice((2 * p + x) * MODES, (2 * p + x + 1) * MODES)
                to = slice((2 * x + part) * MODES, (2 * x + part + 1) * MODES)
                mixed[p, to, :] = got[rows]

    def lon_inverse(kind, out):
        for p in range(OWN):
            table = lonv[kind + (4 if p == 0 else 0)]
            got = matmul(table, mixed[p]).astype(BF16)
            out[p] = got.reshape(LON, TILE, HALF)

    keep_x.wait()
    arrived(0, recv_x)
    lon_forward(recv_x, 0, spec)
    for part in range(2):
        lanes = slice(HALF * part, HALF * part + HALF)
        inner = matmul(spec[...], wide1[:, lanes])
        hyper = jnp.tanh(COEF * (inner + CUBIC * inner * inner * inner))
        act[:, lanes] = (0.5 * inner * (1.0 + hyper)).astype(BF16)
        slope[:, lanes] = 0.5 * (1.0 + hyper) + 0.5 * inner * (1.0 - hyper * hyper) * COEF * (
            1.0 + 3.0 * CUBIC * inner * inner
        )
    for part in range(2):
        lanes = slice(HALF * part, HALF * part + HALF)
        store_mixed(matmul(act[...], wide2[:, lanes]).astype(BF16), part)
    lon_inverse(3, back_x)

    heard(1)
    announce(2)

    spec_t[...] = spec[...].T
    act_t[...] = act[...].T

    def outer(left_t, right, n):
        lane = lax.broadcasted_iota(jnp.int32, (WIDTH, 128), 1)
        for b in range(3):
            low = slice(128 * b, 128 * b + 128)
            high = slice(HALF + 128 * b, HALF + 128 * b + 128)
            columns = jnp.concatenate([right[:, low], right[:, high]], axis=1)
            span = 2 * WIDTH
            top = matmul(left_t[WIDTH * b : WIDTH * b + span, :], columns)
            bottom = matmul(left_t[HALF + WIDTH * b : HALF + WIDTH * b + span, :], columns)
            sums = top[:, :128] + bottom[:, 128:]
            gaps = top[:, 128:] - bottom[:, :128]
            mine = lane < WIDTH - 32 * b
            grads[n, :, low] = jnp.where(mine, sums[:WIDTH], sums[WIDTH:]).astype(BF16)
            grads[n + 1, :, low] = jnp.where(mine, gaps[:WIDTH], gaps[WIDTH:]).astype(BF16)

    def share(k):
        return grads.at[k // 2, pl.ds(pl.multiple_of(lax.rem(k, 2) * 48, 16), 48), :]

    def to_owner(k):
        return pltpu.make_async_remote_copy(
            src_ref=share(k),
            dst_ref=part1.at[e],
            send_sem=sum_out.at[k],
            recv_sem=sum_in.at[e],
            device_id=(dp, device_of(k, u)),
            device_id_type=MESH,
        )

    def each_owner(low, act_on):
        @pl.loop(0, 4)
        def _(i):
            k = low + lax.rem(e + 2 + i, 4)

            @pl.when(k != e)
            def _():
                act_on(to_owner(k))

    def start(copy):
        copy.start()

    keep_y.wait()
    arrived(1, recv_y)
    lon_forward(recv_y, 1, dual)
    outer(act_t, dual, 2)
    each_owner(4, start)
    for part in range(2):
        rows = slice(HALF * part, HALF * part + HALF)
        back = matmul(dual[...], turned2[:, rows])
        pre[:, rows] = (back * slope[:, rows]).astype(BF16)
    outer(spec_t, pre, 0)
    each_owner(0, start)

    for part in range(2):
        rows = slice(HALF * part, HALF * part + HALF)
        store_mixed(matmul(pre[...], turned1[:, rows]).astype(BF16), part)
    lon_inverse(2, back_y)

    def sum_shares():
        part1[e] = share(e)[...]

        @pl.loop(1, 8)
        def _(i):
            k = lax.rem(e + i, 8)
            pltpu.make_async_remote_copy(
                src_ref=part1.at[k],
                dst_ref=part1.at[k],
                send_sem=sum_out.at[k],
                recv_sem=sum_in.at[k],
                device_id=(dp, device_of(k, u)),
                device_id_type=MESH,
            ).wait_recv()

        total = part1[0].astype(F32)
        for k in range(1, 8):
            total = total + part1[k].astype(F32)
        total = total.astype(BF16)
        for t in range(TILES):
            a, b = t // 3, t % 3
            own1[t] = total[16 * a : 16 * a + 16, 128 * b : 128 * b + 128]

    sum_shares()
    heard(2)

    def place_of(t):
        return (16 * t) // TILES

    def reducer(t, h):
        return lax.rem(place_of(t) + 8 * h, 16) * 2 + lax.rem(t, 2)

    def near_reducer(t):
        far = lax.rem(z - place_of(t) + 20, 16) // 8
        return reducer(t, far)

    def to_reducer(t, h):
        return pltpu.make_async_remote_copy(
            src_ref=own1.at[t],
            dst_ref=part2.at[dp],
            send_sem=dp_out.at[2 * t + h],
            recv_sem=dp_in.at[dp],
            device_id=(reducer(t, h), me),
            device_id_type=MESH,
        )

    def each_reducer(act_on):
        @pl.loop(0, 2 * TILES)
        def _(n):
            t, h = n // 2, lax.rem(n, 2)

            @pl.when(dp != reducer(t, h))
            def _():
                act_on(to_reducer(t, h))

    def send_tiles():
        each_reducer(lambda copy: copy.start())

    send_tiles()
    start_all(to_cells, 2, back_x, home_x)
    keep_x = keep_back(back_x, home_x, 2)
    keep_x.start()
    start_all(to_cells, 3, back_y, home_y)
    keep_y = keep_back(back_y, home_y, 3)
    keep_y.start()

    @pl.loop(1, LON)
    def _(i):
        to_mixer(0, send_x, recv_x, i).wait_send()
        to_mixer(1, send_y, recv_y, i).wait_send()

    for low in (0, 4):
        each_owner(low, lambda copy: copy.wait_send())

    def finish_cells(rows, home, out, n):
        for c in range(3):
            lanes = slice(256 * c, 256 * c + 256)
            got = matmul(lati[...], home[:, :, lanes].reshape(LAT * ROWS, 256))
            got = (got * SCALE).astype(BF16).astype(F32) + rows[:, lanes].astype(F32)
            rows[:, lanes] = got.astype(BF16)
        return pltpu.make_async_copy(rows, out, store_sem.at[n])


    spot = lax.rem(z, 8)
    mine = jnp.where(
        lax.rem(spot, 2) == 1,
        (spot + 1) // 2,
        jnp.where(spot == 0, 5 * side, 5 + spot // 2),
    )
    reduces = lax.rem(mine, 2) == side

    def neighbour(i):
        return lax.rem(z + i // 2 + 12, 16) * 2 + lax.rem(i, 2)

    def to_all(i):
        d = neighbour(i)
        return pltpu.make_async_remote_copy(
            src_ref=own3.at[mine],
            dst_ref=own3.at[mine],
            send_sem=cast_out.at[i],
            recv_sem=cast_in.at[mine],
            device_id=(d, me),
            device_id_type=MESH,
        )

    @pl.when(reduces)
    def _():
        part2[dp] = own1[mine]

        @pl.loop(1, dp_count)
        def _(i):
            d = lax.rem(dp + i, dp_count)
            pltpu.make_async_remote_copy(
                src_ref=part2.at[d],
                dst_ref=part2.at[d],
                send_sem=dp_out.at[0],
                recv_sem=dp_in.at[d],
                device_id=(d, me),
                device_id_type=MESH,
            ).wait_recv()

        whole = part2[0].astype(F32)
        for d in range(1, dp_count):
            whole = whole + part2[d].astype(F32)
        own3[mine] = (whole * (1.0 / SAMPLES)).astype(BF16)

        @pl.loop(0, 16)
        def _(i):
            @pl.when(neighbour(i) != dp)
            def _():
                to_all(i).start()

    keep_x.wait()
    arrived(2, home_x)
    store_x = finish_cells(xv, home_x, outx_hbm, 0)
    store_x.start()

    @pl.loop(0, TILES)
    def _(t):
        @pl.when(dp != near_reducer(t))
        def _():
            pltpu.make_async_remote_copy(
                src_ref=own3.at[t],
                dst_ref=own3.at[t],
                send_sem=cast_out.at[0],
                recv_sem=cast_in.at[t],
                device_id=(near_reducer(t), me),
                device_id_type=MESH,
            ).wait_recv()

    twin = me + 1 - 2 * lax.rem(me, 2)

    def to_chips(i):
        return pltpu.make_async_remote_copy(
            src_ref=own3,
            dst_ref=final.at[me],
            send_sem=gather_out.at[i],
            recv_sem=gather_in.at[me],
            device_id=(dp, lax.rem(me + 2 * i, LON)),
            device_id_type=MESH,
        )

    def to_twin(i):
        s = lax.rem(me + 2 * i, LON)
        return pltpu.make_async_remote_copy(
            src_ref=final.at[s],
            dst_ref=final.at[s],
            send_sem=gather_out.at[8 + i],
            recv_sem=gather_in.at[s],
            device_id=(dp, twin),
            device_id_type=MESH,
        )

    def from_peer(s, sender):
        return pltpu.make_async_remote_copy(
            src_ref=final.at[s],
            dst_ref=final.at[s],
            send_sem=gather_out.at[0],
            recv_sem=gather_in.at[s],
            device_id=(dp, sender),
            device_id_type=MESH,
        )

    def gather_start():
        @pl.loop(1, 8)
        def _(i):
            to_chips(8 - i).start()

        final[me] = own3[...]
        to_twin(0).start()

    def gather_forward():
        @pl.loop(1, 8)
        def _(i):
            s = lax.rem(me + 2 * i, LON)
            from_peer(s, s).wait_recv()
            to_twin(i).start()

    def gather_wait():
        @pl.loop(0, 8)
        def _(i):
            from_peer(lax.rem(twin + 2 * i, LON), twin).wait_recv()

    def gather_sent():
        @pl.loop(1, 8)
        def _(i):
            to_chips(i).wait_send()
            to_twin(i).wait_send()

        to_twin(0).wait_send()

    gather_start()

    keep_y.wait()
    arrived(3, home_y)
    store_y = finish_cells(yv, home_y, outy_hbm, 1)
    store_y.start()

    @pl.loop(1, LON)
    def _(i):
        to_cells(2, back_x, home_x, i).wait_send()
        to_cells(3, back_y, home_y, i).wait_send()

    each_reducer(lambda copy: copy.wait_send())

    @pl.when(reduces)
    def _():
        @pl.loop(0, 16)
        def _(i):
            @pl.when(neighbour(i) != dp)
            def _():
                to_all(i).wait_send()

    gather_forward()

    gather_wait()

    store_final = pltpu.make_async_copy(final, grads_hbm, store_sem.at[2])
    store_final.start()

    gather_sent()
    for store in [store_x, store_y, store_final]:
        store.wait()


def deliver(
    x_hbm, y_hbm, grads_hbm, outx_hbm, outy_hbm, grad1_hbm, grad2_hbm,
    xv, yv, final, strip, grad1, grad2, in_sem, out_sem,
):
    loads = [
        pltpu.make_async_copy(grads_hbm, final, in_sem.at[0]),
        pltpu.make_async_copy(x_hbm, xv, in_sem.at[1]),
        pltpu.make_async_copy(y_hbm, yv, in_sem.at[2]),
    ]
    for load in loads:
        load.start()
    stores = [
        pltpu.make_async_copy(xv, outx_hbm, out_sem.at[0]),
        pltpu.make_async_copy(yv, outy_hbm, out_sem.at[1]),
        pltpu.make_async_copy(grad1, grad1_hbm, out_sem.at[2]),
        pltpu.make_async_copy(grad2, grad2_hbm, out_sem.at[3]),
    ]
    loads[0].wait()
    for q in range(4):
        out = (grad1, grad2)[q // 2]
        for v in range(2):
            for t in range(2 * TILES):
                a, b = t // 3, t % 3
                tile = final[4 * q + 2 * v + a // 3, 3 * (a % 3) + b]
                strip[16 * a : 16 * a + 16, 128 * b : 128 * b + 128] = tile.astype(F32)
            for g in range(4):
                out[q % 2, 4 * v + g] = strip[:, WIDTH * g : WIDTH * g + WIDTH]
        if q < 2:
            loads[1 + q].wait()
            stores[q].start()
        if q % 2 == 1:
            stores[2 + q // 2].start()
    for store in stores:
        store.wait()


def on_device(fields, cotangent, first_weight, second_weight):
    dp_count = lax.axis_size("dp")
    rows = ROWS * LAT
    lon = jnp.asarray(lon_matrices(), BF16)
    lat = lat_matrix()
    lat_fwd, lat_inv = jnp.asarray(lat, BF16), jnp.asarray(lat.T.copy(), BF16)
    weight_shape = (2, GROUPS, WIDTH, WIDTH)
    any_spec = pl.BlockSpec(memory_space=pl.ANY)
    dma = pltpu.SemaphoreType.DMA
    cells = pltpu.VMEM((rows, CHANNELS), BF16)
    pairs = pltpu.VMEM((PAIRS, TILE, CHANNELS), BF16)
    lines = pltpu.VMEM((LINES, CHANNELS), BF16)
    blocks = pltpu.VMEM((OWN, LON, TILE, HALF), BF16)
    wide = pltpu.VMEM((CHANNELS, CHANNELS), BF16)
    turned = pltpu.VMEM((CHANNELS, LINES), BF16)
    side = 4 * MODES
    cell_shape = jax.ShapeDtypeStruct((rows, CHANNELS), BF16)
    grad_shape = jax.ShapeDtypeStruct(weight_shape, F32)
    final_shape = (LON, TILES, 16, 128)
    results = pl.pallas_call(
        kernel,
        out_shape=(cell_shape, cell_shape, jax.ShapeDtypeStruct(final_shape, BF16)),
        in_specs=[any_spec] * 7,
        out_specs=(any_spec,) * 3,
        scratch_shapes=[
            cells, cells,
            pltpu.VMEM(weight_shape, BF16), pltpu.VMEM(weight_shape, BF16),
            pltpu.VMEM((8, side, side), BF16),
            pltpu.VMEM((rows, rows), BF16), pltpu.VMEM((rows, rows), BF16),
            pairs, pairs, blocks, blocks, blocks, blocks, pairs, pairs,
            wide, wide, wide, wide,
            pltpu.VMEM((2, HALF, HALF), F32),
            lines, lines, lines, lines,
            pltpu.VMEM((LINES, CHANNELS), F32),
            pltpu.VMEM((OWN, side, HALF), BF16),
            turned, turned,
            pltpu.VMEM((4, WIDTH, HALF), BF16),
            pltpu.VMEM((8, 48, HALF), BF16),
            pltpu.VMEM((TILES, 16, 128), BF16),
            pltpu.VMEM((dp_count, 16, 128), BF16),
            pltpu.VMEM((TILES, 16, 128), BF16),
            pltpu.VMEM((LON, TILES, 16, 128), BF16),
            dma((8,)), dma((3,)), dma((4,)), dma((4, LON)), dma((4, LON)),
            dma((8,)), dma((8,)), dma((2 * TILES,)), dma((dp_count,)),
            dma((16,)), dma((TILES,)), dma((LON,)), dma((LON,)),
            pltpu.SemaphoreType.REGULAR((3,)),
        ],
        compiler_params=pltpu.CompilerParams(
            collective_id=0, has_side_effects=True, vmem_limit_bytes=63 << 20
        ),
    )(
        fields.reshape(rows, CHANNELS), cotangent.reshape(rows, CHANNELS),
        first_weight, second_weight, lon, lat_fwd, lat_inv,
    )
    wave, pull, grad1, grad2 = pl.pallas_call(
        deliver,
        out_shape=(cell_shape, cell_shape, grad_shape, grad_shape),
        in_specs=[any_spec] * 3,
        out_specs=(any_spec,) * 4,
        scratch_shapes=[
            cells, cells, pltpu.VMEM(final_shape, BF16), pltpu.VMEM((WIDTH, HALF), F32),
            pltpu.VMEM(weight_shape, F32), pltpu.VMEM(weight_shape, F32),
            dma((3,)), dma((4,)),
        ],
        compiler_params=pltpu.CompilerParams(vmem_limit_bytes=63 << 20),
    )(*results)
    shape = (1, ROWS, LAT, CHANNELS)
    return wave.reshape(shape), pull.reshape(shape), grad1, grad2


def solution(mesh):
    placed = (P("dp", "lon", None, None), P("dp", "lon", None, None), P(), P())
    return jax.shard_map(
        on_device, mesh=mesh, in_specs=placed, out_specs=placed, check_vma=False
    )
```
